32 devices in a mesh: long: 8 (over y, x, core), short: 4 (over z).
Axes of the slice: x: 2, y: 2, z: 4, core: 2. Of those that a mesh axis runs over, the one named last changes fastest.
Arguments:
- transition: float32 [64, 384, 384], P(('long', 'short')), may hold values from 0 to 1
- innovation: float32 [64, 384], P(('long', 'short')), may hold values from 20 to 80
- observation: float32 [64, 384], P(('long', 'short')), may hold values from 0.05 to 0.5
- effects: float32 [64, 384, 384], P(('long', 'short')), may hold values from -0.0045 to 0.0045
- prior: float32 [384], replicated, may hold values from 0.5 to 2
- right_side: float32 [64, 384, 128], P(('long', 'short')), may hold values from -3 to 3
- tip_right: float32 [384, 128], replicated, may hold values from -6 to 6
Outputs:
- solution: float32 [64, 384, 128], P(('long', 'short'))
- tip_solution: float32 [384, 128], replicated
The draws below stay inside these ranges and needn't reach their ends.
All inputs are finite; a program needn't handle non-finite values.
Results may differ from the reference program's by a relative error of at most 0.0003.
Values sent between devices are 32-bit elements; how exact they have to be, the bound alone decides.
A program may use at most 256 MiB of HBM per device.

```python
import math
import jax
import jax.numpy as jnp
from jax import lax

B = 384
K = 384
NR = 128
NT = 64


def draw_transition(key, part):
    rate_key, link_key = jax.random.split(jax.random.fold_in(key, 11))
    persistence = jax.random.uniform(rate_key, (NT, B), jnp.float32, 0.9, 0.995)
    ahead_rate = jax.random.uniform(link_key, (NT, B), jnp.float32, 0.05, 0.2)
    behind_rate = jnp.roll(ahead_rate, 1, axis=1)
    identity = jnp.eye(B, dtype=jnp.float32)
    ahead_matrix = jnp.roll(identity, 1, axis=1)
    behind_matrix = ahead_matrix.T
    mixing = (1.0 - ahead_rate - behind_rate)[:, :, None] * identity[None] + ahead_rate[:, :, None] * ahead_matrix[None] + behind_rate[:, :, None] * behind_matrix[None]
    return (persistence[:, :, None] * mixing).astype(jnp.float32)


def draw_effects(key, part):
    common_key, block_key = jax.random.split(jax.random.fold_in(key, 23))
    common_part = 0.0013 * jax.random.normal(common_key, (B, K), jnp.float32)
    block_part = 0.0006 * jax.random.normal(block_key, (NT, B, K), jnp.float32)
    loading = common_part[None] + block_part
    return jnp.clip(loading, -0.0045, 0.0045).astype(jnp.float32)


def level_of(own_key, shape, shards, least, largest):
    loudness, own = 1.0, jax.random.fold_in(own_key, 6)
    for axis_at, shards_of in shards:
        steps = jnp.exp(jax.random.uniform(jax.random.fold_in(own, axis_at), (shards_of,), jnp.float32, least / len(shards), largest / len(shards)))
        loudness = loudness * jnp.repeat(steps, shape[axis_at] // shards_of).reshape([-1 if axis == axis_at else 1 for axis in range(len(shape))])
    return loudness


def scatter_about(key, dims, deviation, bound, shards=(), held_as=jnp.bfloat16):
    values = jax.random.normal(key, dims, jnp.float32) * deviation
    if len(shards) > 0:
        values = level_of(key, dims, shards, -0.22, 0.18) * values
    return jnp.clip(values, min=-bound, max=bound).astype(held_as)


def setup_inputs(seed: int = 0) -> dict:
    arg_keys = jax.random.split(jax.random.key(seed), 8)
    return {
        "transition": draw_transition(jax.random.fold_in(arg_keys[7], 71), 0),
        "innovation": jnp.clip(jnp.exp(math.log(80.0) - 1.3862944 * jax.random.uniform(arg_keys[1], (NT, B), jnp.float32) ** level_of(arg_keys[1], (NT, B), ((0, 32),), -0.2, 0.2)), 20.0, 80.0),
        "observation": jnp.clip(jnp.exp(math.log(0.5) - 2.3025851 * jax.random.uniform(arg_keys[2], (NT, B), jnp.float32) ** level_of(arg_keys[2], (NT, B), ((0, 32),), -0.2, 0.2)), 0.05, 0.5),
        "effects": draw_effects(jax.random.fold_in(arg_keys[7], 71), 0),
        "prior": jnp.clip(jnp.exp(jax.random.uniform(arg_keys[4], (K,), jnp.float32, math.log(0.5), math.log(2.0))), 0.5, 2.0),
        "right_side": scatter_about(arg_keys[5], (NT, B, NR), 0.5, 3.0, ((0, 32),), jnp.float32),
        "tip_right": scatter_about(arg_keys[6], (K, NR), 1.0, 6.0, (), jnp.float32),
    }


HIGHEST = lax.Precision.HIGHEST

def gram_prod(left, right):
    return jnp.einsum('ji,jk->ik', left, right, precision=HIGHEST)

def mat_prod(left, right):
    return jnp.matmul(left, right, precision=HIGHEST)

def solve_lower(factor, values):
    return jax.scipy.linalg.solve_triangular(factor, values, lower=True)

def solve_upper(factor, values):
    return jax.scipy.linalg.solve_triangular(factor, values, lower=True, trans=1)

def reference(transition, innovation, observation, effects, prior, right_side, tip_right):
    block_count, node_width = innovation.shape
    tip_width = prior.shape[0]
    side_count = right_side.shape[2]
    identity = jnp.eye(node_width, dtype=jnp.float32)
    weighted_trans = innovation[:, :, None] * transition
    weighted_effect = innovation[:, :, None] * effects

    def successor(items):
        trans_block, trans_weighted, effect_weighted = items
        return (gram_prod(trans_block, trans_weighted), gram_prod(trans_block, effect_weighted))
    succ_diag, succ_arrow = lax.map(successor, (transition, weighted_trans, weighted_effect))
    zero_square = jnp.zeros((1, node_width, node_width), jnp.float32)
    zero_arrow = jnp.zeros((1, node_width, tip_width), jnp.float32)
    next_diag = jnp.concatenate([succ_diag[1:], zero_square], axis=0)
    next_arrow = jnp.concatenate([succ_arrow[1:], zero_arrow], axis=0)
    keep_mask = jnp.where(jnp.arange(block_count) == 0, 0.0, 1.0).astype(jnp.float32)
    couple = -weighted_trans * keep_mask[:, None, None]
    diag_block = (innovation + observation)[:, :, None] * identity + next_diag
    arrow = -weighted_effect + next_arrow
    tip_block = jnp.diag(prior) + jnp.einsum('tji,tjk->ik', effects, weighted_effect, precision=HIGHEST)
    columns = jnp.concatenate([arrow, right_side], axis=2)

    def forward(carry, items):
        factor_prev, solved_prev, tip_terms = carry
        diag_item, couple_item, column_item = items
        link = solve_lower(factor_prev, couple_item.T)
        factor = jnp.linalg.cholesky(diag_item - gram_prod(link, link))
        solved = solve_lower(factor, column_item - gram_prod(link, solved_prev))
        tip_terms = tip_terms + gram_prod(solved[:, :tip_width], solved)
        return ((factor, solved, tip_terms), (factor, link, solved))
    start = (identity, jnp.zeros((node_width, tip_width + side_count), jnp.float32), jnp.zeros((tip_width, tip_width + side_count), jnp.float32))
    final_carry, stored = lax.scan(forward, start, (diag_block, couple, columns))
    tip_terms = final_carry[2]
    factors, links, solved_all = stored
    tip_factor = jnp.linalg.cholesky(tip_block - tip_terms[:, :tip_width])
    tip_solution = solve_upper(tip_factor, solve_lower(tip_factor, tip_right - tip_terms[:, tip_width:]))
    next_links = jnp.concatenate([links[1:], zero_square], axis=0)

    def backward(later, items):
        factor, link_next, solved = items
        value = solved[:, tip_width:] - mat_prod(solved[:, :tip_width], tip_solution) - mat_prod(link_next, later)
        current = solve_upper(factor, value)
        return (current, current)
    last_value, solution = lax.scan(backward, jnp.zeros((node_width, side_count), jnp.float32), (factors, next_links, solved_all), reverse=True)
    return (solution, tip_solution)
```

```python
import functools

import jax
import jax.numpy as jnp
from jax import lax
from jax.experimental import pallas as pl
from jax.experimental.pallas import tpu as pltpu
from jax.sharding import PartitionSpec as P

AXES = ("long", "short")
PREC = lax.Precision.HIGHEST
LANES = 128
SUBLANES = 8
MESH = pl.DeviceIdType.MESH
F32 = jnp.float32


def dot(left, right):
    return jnp.dot(left, right, precision=PREC, preferred_element_type=F32)


def gram(left, right):
    return lax.dot_general(
        left, right, (((0,), (0,)), ((), ())), precision=PREC, preferred_element_type=F32
    )


def inverse_two(a, b, c):
    inv = 1.0 / (a * c - b * b)
    return c * inv, -(b * inv), a * inv


def pivot_four(tiles, first, lane, sub):
    group, row = divmod(first, SUBLANES)
    shape = (SUBLANES, LANES)
    cols = [
        [jnp.broadcast_to(t[:, first + k : first + k + 1], shape) for t in tiles] for k in range(4)
    ]

    def entry(i, k):
        return cols[k][group][row + i : row + i + 1, :]

    a00, a01, a11 = inverse_two(entry(0, 0), entry(0, 1), entry(1, 1))
    b00, b01, b10, b11 = entry(0, 2), entry(0, 3), entry(1, 2), entry(1, 3)
    m00, m01 = a00 * b00 + a01 * b10, a00 * b01 + a01 * b11
    m10, m11 = a01 * b00 + a11 * b10, a01 * b01 + a11 * b11
    s00, s01, s11 = inverse_two(
        entry(2, 2) - (b00 * m00 + b10 * m10),
        entry(2, 3) - (b00 * m01 + b10 * m11),
        entry(3, 3) - (b01 * m01 + b11 * m11),
    )
    u00, u01 = m00 * s00 + m01 * s01, m00 * s01 + m01 * s11
    u10, u11 = m10 * s00 + m11 * s01, m10 * s01 + m11 * s11
    t01 = a01 + (u00 * m10 + u01 * m11)
    pivot_inverse = (
        (a00 + (u00 * m00 + u01 * m01), t01, -u00, -u01),
        (t01, a11 + (u10 * m10 + u11 * m11), -u10, -u11),
        (-u00, -u10, s00, s01),
        (-u01, -u11, s01, s11),
    )
    inside = jnp.logical_and(lane >= first, lane < first + 4)
    rows = [
        jnp.where(
            inside[:1],
            jnp.where(lane[:1] == first + k, 1.0, 0.0),
            tiles[group][row + k : row + k + 1, :],
        )
        for k in range(4)
    ]
    scaled = [
        jnp.broadcast_to(
            (p[0] * rows[0] + p[1] * rows[1]) + (p[2] * rows[2] + p[3] * rows[3]), shape
        )
        for p in pivot_inverse
    ]
    out = []
    for place, tile in enumerate(tiles):
        new = jnp.where(inside, 0.0, tile)
        for k in range(4):
            new = new - cols[k][place] * scaled[k]
        if place == group:
            for k in range(4):
                new = jnp.where(sub == row + k, scaled[k], new)
        out.append(new)
    return out


def invert(o_ref):
    width = o_ref.shape[0]
    lane = lax.broadcasted_iota(jnp.int32, (SUBLANES, LANES), 1)
    sub = lax.broadcasted_iota(jnp.int32, (SUBLANES, LANES), 0)

    def step(k, carry):
        at = pl.multiple_of(k * LANES, LANES)
        here = pl.ds(at, LANES)
        tiles = [
            o_ref[pl.ds(pl.multiple_of(at + SUBLANES * g, SUBLANES), SUBLANES), here]
            for g in range(LANES // SUBLANES)
        ]
        for first in range(0, LANES, 4):
            tiles = pivot_four(tiles, first, lane, sub)
        pivot = jnp.concatenate(tiles, axis=0)
        rows = o_ref[here, :]
        columns = o_ref[:, here]
        scaled = dot(pivot, rows)
        o_ref[here, :] = scaled
        o_ref[here, here] = pivot
        scaled = o_ref[here, :]
        o_ref[:, here] = jnp.zeros((width, LANES), F32)
        o_ref[...] = o_ref[...] - dot(columns, scaled)
        o_ref[here, :] = scaled
        return carry

    lax.fori_loop(0, width // LANES, step, 0)


def host_side(level, segment):
    if level == 0:
        return 1 - lax.rem(segment // 2, 2)
    if level == 1:
        return lax.rem(segment, 2)
    return 0


def host_of(level, segment):
    for low in reversed(range(level)):
        segment = 2 * segment + host_side(low, segment)
    return segment


def choose(values, index):
    picked = values[0]
    for k in range(1, len(values)):
        picked = jnp.where(index == k, values[k], picked)
    return picked


def column_of(row, width):
    turned = jnp.broadcast_to(row, (LANES, row.shape[1])).T
    return jnp.concatenate([turned] * (width // LANES), axis=1)


def diagonal(row):
    n = row.shape[1]
    at = lax.broadcasted_iota(jnp.int32, (n, n), 0)
    across = lax.broadcasted_iota(jnp.int32, (n, n), 1)
    return jnp.where(at == across, jnp.broadcast_to(row, (n, n)), 0.0)


def kernel(
    levels, shorts,
    trans, innov, observ, effects, prior, right, tip_right,
    out, tip_out,
    dd, ab, tip, work, abm, xs, ys, yab,
    near_d, near_ab, far_d, far_ab, got_tip, sol, tip_sol,
    send_sem, recv_sem, back_send, back_recv,
):
    n = trans.shape[1]
    k = effects.shape[2]
    m = right.shape[2]
    me = lax.axis_index("long") * shorts + lax.axis_index("short")

    segs = [me // (1 << v) for v in range(levels + 1)]
    halves = [lax.rem(s, 2) for s in segs]
    active = [host_of(v, segs[v]) == me for v in range(levels + 1)]
    partners = [host_of(v, segs[v] + 1 - 2 * halves[v]) for v in range(levels)]
    hosting = [active[v + 1] for v in range(levels)]
    sending = [jnp.logical_and(active[v], jnp.logical_not(active[v + 1])) for v in range(levels)]

    def place(position):
        return (position // shorts, lax.rem(position, shorts))

    barrier = pltpu.get_barrier_semaphore()
    for v in range(levels):
        @pl.when(active[v])
        def _():
            pl.semaphore_signal(barrier, inc=1, device_id=place(partners[v]), device_id_type=MESH)

    def forward_copy(what, v, side, far, target):
        parts = (
            (dd.at[side], near_d.at[v]),
            (xs.at[v + 1, far], xs.at[v + 1, far]),
            (ab.at[side], near_ab.at[v]),
            (dd.at[far], far_d.at[v]),
            (ab.at[far], far_ab.at[v]),
            (tip, got_tip.at[v]),
        )
        return pltpu.make_async_remote_copy(
            src_ref=parts[what][0],
            dst_ref=parts[what][1],
            send_sem=send_sem.at[what],
            recv_sem=recv_sem.at[v, what],
            device_id=place(target),
            device_id_type=MESH,
        )

    first = jnp.where(me == 0, 0.0, 1.0).astype(F32)
    trans_now = trans[0] * first
    weight_now = column_of(innov[0:1, :], n)
    weight_next = column_of(innov[1:2, :], n)
    scaled_next = weight_next * trans[1]
    work[...] = diagonal(innov[0:1, :] + observ[0:1, :]) + gram(trans[1], scaled_next)
    xs[0, 1] = -(scaled_next.T)
    scaled_now = weight_now * trans_now
    xs[0, 0] = -scaled_now
    dd[0] = gram(trans_now, scaled_now)
    dd[1] = diagonal(innov[1:2, :] + observ[1:2, :])

    count = active[0].astype(jnp.int32)
    for v in range(1, levels):
        count = count + active[v].astype(jnp.int32)
    pl.semaphore_wait(barrier, count)

    def stage(s, carry):
        last = levels
        below = jnp.maximum(s - 1, 0)
        half = choose(halves, below)
        near_now = 1 - half
        far_next = choose(halves, jnp.minimum(s, last))
        near_next = 1 - far_next
        runs = choose(active + [active[levels]] * 2, s)
        sends = jnp.logical_and(s < last, choose(sending + [sending[0]], jnp.minimum(s, last)))
        target = choose(partners, jnp.minimum(s, last - 1))
        merges = jnp.logical_and(s > 0, s <= last)

        def arrived(what):
            forward_copy(what, below, near_now, 1 - half, me).wait_recv()

        @pl.when(runs)
        def _():
            @pl.when(merges)
            def _():
                arrived(0)
                work[...] = dd[near_now] + near_d[below]

            @pl.when(s == last + 1)
            def _():
                work[...] = dd[1]

            @pl.when(s == last + 2)
            def _():
                work[...] = tip[:, :k] + diagonal(prior[...])

            invert(work)

            @pl.when(s <= last)
            def _():
                @pl.when(merges)
                def _():
                    arrived(1)
                    arrived(2)
                    abm[...] = ab[near_now] + near_ab[below]
                    arrived(3)
                    dd[near_now] = far_d[below]
                    arrived(4)
                    ab[near_now] = far_ab[below]

                ys[near_next] = dot(work[...], xs[s, near_next])
                dd[near_next] = dd[near_next] - gram(xs[s, near_next], ys[near_next])

                @pl.when(sends)
                def _():
                    forward_copy(0, s, near_next, far_next, target).start()

                ys[far_next] = dot(work[...], xs[s, far_next])

                @pl.when(s < last)
                def _():
                    xs[s + 1, far_next] = -gram(xs[s, near_next], ys[far_next])

                @pl.when(sends)
                def _():
                    forward_copy(1, s, near_next, far_next, target).start()

                @pl.when(s == 0)
                def _():
                    loaded_now = weight_col(0) * effects[0]
                    loaded_next = weight_col(1) * effects[1]
                    abm[:, :k] = gram(trans[1], loaded_next) - loaded_now
                    abm[:, k:] = right[0]
                    ab[0, :, :k] = gram(trans[0] * first, loaded_now)
                    ab[0, :, k:] = jnp.zeros((n, m), F32)
                    ab[1, :, :k] = -loaded_next
                    ab[1, :, k:] = right[1]
                    tip[:, :k] = gram(effects[0], loaded_now) + gram(effects[1], loaded_next)
                    tip[:, k:] = jnp.zeros((k, m), F32)

                yab[s] = dot(work[...], abm[...])
                ab[near_next] = ab[near_next] - gram(xs[s, near_next], yab[s])

                @pl.when(sends)
                def _():
                    forward_copy(2, s, near_next, far_next, target).start()

                dd[far_next] = dd[far_next] - gram(xs[s, far_next], ys[far_next])

                @pl.when(sends)
                def _():
                    forward_copy(3, s, near_next, far_next, target).start()

                ab[far_next] = ab[far_next] - gram(xs[s, far_next], yab[s])

                @pl.when(sends)
                def _():
                    forward_copy(4, s, near_next, far_next, target).start()

                tip[...] = tip[...] - gram(abm[:, :k], yab[s])
                xs[s, 0] = ys[0]
                xs[s, 1] = ys[1]

            @pl.when(s == last + 1)
            def _():
                yab[s] = dot(work[...], ab[1])
                tip[...] = tip[...] - gram(ab[1, :, :k], yab[s])

            @pl.when(jnp.logical_or(sends, s == last + 1))
            def _():
                for v in range(levels):
                    @pl.when(jnp.logical_and(hosting[v], v < s))
                    def _():
                        forward_copy(5, v, 0, 1, me).wait_recv()
                        tip[...] = tip[...] + got_tip[v]

            @pl.when(sends)
            def _():
                forward_copy(5, s, near_next, far_next, target).start()

            @pl.when(s == last + 2)
            def _():
                found = dot(work[...], tip[:, k:] + tip_right[...])
                tip_sol[...] = found
                sol[levels, 1] = yab[last + 1, :, k:] - dot(yab[last + 1, :, :k], found)
                sol[levels, 0] = jnp.zeros((n, m), F32)

        return carry

    def weight_col(t):
        return column_of(innov[t : t + 1, :], k)

    lax.fori_loop(0, levels + 3, stage, 0)

    def back_copy(what, v, half, target):
        other = 1 - half
        src = (tip_sol, sol.at[v + 1, other], sol.at[v, other])[what]
        dst = (tip_sol, sol.at[v, other], sol.at[v, half])[what]
        return pltpu.make_async_remote_copy(
            src_ref=src,
            dst_ref=dst,
            send_sem=back_send.at[v, what],
            recv_sem=back_recv.at[what],
            device_id=place(target),
            device_id_type=MESH,
        )

    def back(i, carry):
        v = levels - 1 - i
        half = choose(halves, v)
        hosts = choose(hosting, v)
        waits = choose(sending, v)
        target = choose(partners, v)

        @pl.when(hosts)
        def _():
            back_copy(0, v, half, target).start()
            back_copy(1, v, half, target).start()
            value = yab[v + 1, :, k:] - dot(yab[v + 1, :, :k], tip_sol[...])
            value = value - dot(xs[v + 1, 0], sol[v + 1, 0])
            sol[v, 1 - half] = value - dot(xs[v + 1, 1], sol[v + 1, 1])
            back_copy(2, v, half, target).start()
            sol[v, half] = sol[v + 1, half]

        @pl.when(waits)
        def _():
            for what in range(3):
                back_copy(what, v, 1 - half, me).wait_recv()

        return carry

    lax.fori_loop(0, levels, back, 0)

    value = yab[0, :, k:] - dot(yab[0, :, :k], tip_sol[...])
    value = value - dot(xs[0, 0], sol[0, 0])
    out[0] = value - dot(xs[0, 1], sol[0, 1])
    out[1] = sol[0, 1]
    tip_out[...] = tip_sol[...]

    for v in range(levels):
        @pl.when(sending[v])
        def _():
            for what in range(6):
                forward_copy(what, v, 1 - halves[v], halves[v], partners[v]).wait_send()

        @pl.when(hosting[v])
        def _():
            for what in range(3):
                back_copy(what, v, halves[v], partners[v]).wait_send()


def body(transition, innovation, observation, effects, prior, right_side, tip_right):
    blocks, n = innovation.shape
    k = prior.shape[0]
    m = right_side.shape[2]
    shorts = lax.axis_size("short")
    total = lax.axis_size(AXES)
    levels = total.bit_length() - 1
    assert blocks == 2 and total == 1 << levels
    vmem = pl.BlockSpec(memory_space=pltpu.VMEM)
    wide = k + m
    return pl.pallas_call(
        functools.partial(kernel, levels, shorts),
        out_shape=(
            jax.ShapeDtypeStruct(right_side.shape, F32),
            jax.ShapeDtypeStruct(tip_right.shape, F32),
        ),
        in_specs=[vmem] * 7,
        out_specs=(vmem, vmem),
        scratch_shapes=[
            pltpu.VMEM((2, n, n), F32),
            pltpu.VMEM((2, n, wide), F32),
            pltpu.VMEM((k, wide), F32),
            pltpu.VMEM((n, n), F32),
            pltpu.VMEM((n, wide), F32),
            pltpu.VMEM((levels + 1, 2, n, n), F32),
            pltpu.VMEM((2, n, n), F32),
            pltpu.VMEM((levels + 2, n, wide), F32),
            pltpu.VMEM((levels, n, n), F32),
            pltpu.VMEM((levels, n, wide), F32),
            pltpu.VMEM((levels, n, n), F32),
            pltpu.VMEM((levels, n, wide), F32),
            pltpu.VMEM((levels, k, wide), F32),
            pltpu.VMEM((levels + 1, 2, n, m), F32),
            pltpu.VMEM((k, m), F32),
            pltpu.SemaphoreType.DMA((6,)),
            pltpu.SemaphoreType.DMA((levels, 6)),
            pltpu.SemaphoreType.DMA((levels, 3)),
            pltpu.SemaphoreType.DMA((3,)),
        ],
        compiler_params=pltpu.CompilerParams(
            collective_id=0, has_side_effects=True, vmem_limit_bytes=67000000
        ),
        name="arrow_solve",
    )(transition, innovation, observation, effects, prior.reshape(1, k), right_side, tip_right)


def solution(mesh):
    placed = (
        P(AXES, None, None),
        P(AXES, None),
        P(AXES, None),
        P(AXES, None, None),
        P(),
        P(AXES, None, None),
        P(),
    )
    return jax.shard_map(
        body,
        mesh=mesh,
        in_specs=placed,
        out_specs=(P(AXES, None, None), P()),
        check_vma=False,
    )
```

```python
import functools

import jax
import jax.numpy as jnp
from jax import lax
from jax.experimental import pallas as pl
from jax.experimental.pallas import tpu as pltpu
from jax.sharding import PartitionSpec as P

AXES = ("long", "short")
PREC = lax.Precision.HIGHEST
LANES = 128
SUBLANES = 8
MESH = pl.DeviceIdType.MESH
F32 = jnp.float32


def dot(left, right):
    return jnp.dot(left, right, precision=PREC, preferred_element_type=F32)


def gram(left, right):
    return lax.dot_general(
        left, right, (((0,), (0,)), ((), ())), precision=PREC, preferred_element_type=F32
    )


def inverse_two(a, b, c):
    inv = 1.0 / (a * c - b * b)
    return c * inv, -(b * inv), a * inv


def pivot_four(tiles, first, lane, sub):
    group, row = divmod(first, SUBLANES)
    shape = (SUBLANES, LANES)
    cols = [
        [jnp.broadcast_to(t[:, first + k : first + k + 1], shape) for t in tiles] for k in range(4)
    ]

    def entry(i, k):
        return cols[k][group][row + i : row + i + 1, :]

    a00, a01, a11 = inverse_two(entry(0, 0), entry(0, 1), entry(1, 1))
    b00, b01, b10, b11 = entry(0, 2), entry(0, 3), entry(1, 2), entry(1, 3)
    m00, m01 = a00 * b00 + a01 * b10, a00 * b01 + a01 * b11
    m10, m11 = a01 * b00 + a11 * b10, a01 * b01 + a11 * b11
    s00, s01, s11 = inverse_two(
        entry(2, 2) - (b00 * m00 + b10 * m10),
        entry(2, 3) - (b00 * m01 + b10 * m11),
        entry(3, 3) - (b01 * m01 + b11 * m11),
    )
    u00, u01 = m00 * s00 + m01 * s01, m00 * s01 + m01 * s11
    u10, u11 = m10 * s00 + m11 * s01, m10 * s01 + m11 * s11
    t01 = a01 + (u00 * m10 + u01 * m11)
    pivot_inverse = (
        (a00 + (u00 * m00 + u01 * m01), t01, -u00, -u01),
        (t01, a11 + (u10 * m10 + u11 * m11), -u10, -u11),
        (-u00, -u10, s00, s01),
        (-u01, -u11, s01, s11),
    )
    inside = jnp.logical_and(lane >= first, lane < first + 4)
    rows = [
        jnp.where(
            inside[:1],
            jnp.where(lane[:1] == first + k, 1.0, 0.0),
            tiles[group][row + k : row + k + 1, :],
        )
        for k in range(4)
    ]
    scaled = [
        jnp.broadcast_to(
            (p[0] * rows[0] + p[1] * rows[1]) + (p[2] * rows[2] + p[3] * rows[3]), shape
        )
        for p in pivot_inverse
    ]
    out = []
    for place, tile in enumerate(tiles):
        new = jnp.where(inside, 0.0, tile)
        for k in range(4):
            new = new - cols[k][place] * scaled[k]
        if place == group:
            for k in range(4):
                new = jnp.where(sub == row + k, scaled[k], new)
        out.append(new)
    return out


def pivot_inverse(block):
    lane = lax.broadcasted_iota(jnp.int32, (SUBLANES, LANES), 1)
    sub = lax.broadcasted_iota(jnp.int32, (SUBLANES, LANES), 0)
    tiles = [block[SUBLANES * g : SUBLANES * (g + 1), :] for g in range(LANES // SUBLANES)]
    for first in range(0, LANES, 4):
        tiles = pivot_four(tiles, first, lane, sub)
    return jnp.concatenate(tiles, axis=0)


def span(j):
    return pl.ds(j * LANES, LANES)


def sweep(w, slot, j, pivot):
    here = span(j)
    width = w.shape[1]
    columns = w[slot, :, here]
    w[slot, here, :] = dot(pivot, w[slot, here, :])
    w[slot, here, here] = pivot
    scaled = w[slot, here, :]
    w[slot, :, here] = jnp.zeros((width, LANES), F32)
    w[slot] = w[slot] - dot(columns, scaled)
    w[slot, here, :] = scaled


def next_pivot_block(w, slot, j, pivot):
    after = span(j + 1)
    scaled = dot(pivot, w[slot, span(j), after])
    return w[slot, after, after] - dot(w[slot, after, span(j)], scaled)


def host_side(segment):
    return 1 - lax.rem(segment, 2)


def host_of(level, segment):
    for _ in range(level):
        segment = 2 * segment + host_side(segment)
    return segment


def choose(values, index):
    picked = values[0]
    for k in range(1, len(values)):
        picked = jnp.where(index == k, values[k], picked)
    return picked


def column_of(row, width):
    turned = jnp.broadcast_to(row, (LANES, row.shape[1])).T
    return jnp.concatenate([turned] * (width // LANES), axis=1)


def diagonal(row):
    n = row.shape[1]
    at = lax.broadcasted_iota(jnp.int32, (n, n), 0)
    across = lax.broadcasted_iota(jnp.int32, (n, n), 1)
    return jnp.where(at == across, jnp.broadcast_to(row, (n, n)), 0.0)


def kernel(
    levels, shorts,
    trans, innov, observ, effects, prior, right, tip_right,
    out, tip_out,
    dd, ab, tip, work, abm, xs, ys,
    near_d, near_ab, far_d, far_ab, got_tip, sol, tip_sol, tip_rhs,
    send_sem, recv_sem, back_send, back_recv,
):
    n = trans.shape[1]
    k = effects.shape[2]
    m = right.shape[2]
    last = levels
    steps = n // LANES
    me = lax.axis_index("long") * shorts + lax.axis_index("short")

    segs = [me // (1 << v) for v in range(levels + 1)]
    halves = [lax.rem(s, 2) for s in segs]
    active = [host_of(v, segs[v]) == me for v in range(levels + 1)]
    partners = [host_of(v, segs[v] + 1 - 2 * halves[v]) for v in range(levels)]
    hosting = [active[v + 1] for v in range(levels)]
    sending = [jnp.logical_and(active[v], jnp.logical_not(active[v + 1])) for v in range(levels)]

    def place(position):
        return (position // shorts, lax.rem(position, shorts))

    barrier = pltpu.get_barrier_semaphore()
    for v in range(levels):
        @pl.when(active[v])
        def _():
            pl.semaphore_signal(barrier, inc=1, device_id=place(partners[v]), device_id_type=MESH)

    top = pl.ds(0, LANES)
    beyond = pl.ds(LANES, n - LANES)

    def forward_copy(what, v, near, far, target):
        src, dst = (
            lambda: (dd.at[near, top, top], near_d.at[v, top, top]),
            lambda: (dd.at[near, top, beyond], near_d.at[v, top, beyond]),
            lambda: (dd.at[near, beyond], near_d.at[v, beyond]),
            lambda: (xs.at[v + 1, far], xs.at[v + 1, far]),
            lambda: (ab.at[near], near_ab.at[v]),
            lambda: (dd.at[far], far_d.at[v]),
            lambda: (ab.at[far], far_ab.at[v]),
            lambda: (tip, got_tip.at[v]),
        )[what]()
        return pltpu.make_async_remote_copy(
            src_ref=src,
            dst_ref=dst,
            send_sem=send_sem.at[what],
            recv_sem=recv_sem.at[v, what],
            device_id=place(target),
            device_id_type=MESH,
        )

    first = jnp.where(me == 0, 0.0, 1.0).astype(F32)

    def weight(t, width):
        return column_of(innov[t : t + 1, :], width)

    work[0] = diagonal(innov[0:1, :] + observ[0:1, :]) + gram(trans[1], weight(1, n) * trans[1])

    count = active[0].astype(jnp.int32)
    for v in range(1, levels):
        count = count + active[v].astype(jnp.int32)
    pl.semaphore_wait(barrier, count)

    runs_at = [active[0]] + active + [active[last]]
    hosts_at = active + [active[last]] * 2

    def stage(s, carry):
        slot = lax.rem(s, 2)
        old = 1 - slot
        hosts = choose(hosts_at, s)
        merges = jnp.logical_and(hosts, jnp.logical_and(s > 0, s <= last))
        below = jnp.clip(s - 1, 0, last - 1)
        fs = jnp.clip(s - 1, 0, last)
        real = jnp.logical_and(s > 0, s <= last + 1)
        fed = jnp.logical_and(s > 1, s <= last + 1)
        fed_from = jnp.clip(fs - 1, 0, last - 1)
        inner = choose(halves, fs)
        outer = 1 - inner
        sent = jnp.logical_and(s > 0, choose(sending, below))
        sent = jnp.logical_and(sent, s <= last)
        sent_to = choose(partners, below)
        keep = jnp.where(real, jnp.where(fs == 0, last, fs - 1), last + 2)

        def send(what):
            @pl.when(sent)
            def _():
                forward_copy(what, below, outer, inner, sent_to).start()

        def arrived(what, v):
            forward_copy(what, v, 0, 1 - choose(halves, v), me).wait_recv()

        @pl.when(choose(runs_at, s))
        def _():
            near = 1 - choose(halves, below)

            @pl.when(merges)
            def _():
                arrived(0, below)
                work[slot, top, top] = dd[near, top, top] + near_d[below, top, top]

            @pl.when(s == last + 1)
            def _():
                work[slot] = dd[1]

            @pl.when(s == last + 2)
            def _():
                work[slot] = tip[:, :k] + diagonal(prior[...])
                tip_rhs[...] = tip[:, k:] + tip_right[...]

            @pl.when(fed)
            def _():
                arrived(3, fed_from)

            pivot = pivot_inverse(work[slot, top, top])
            y_in = dot(work[old], xs[fs, inner])
            ys[1] = y_in
            xs[fs + 1, inner] = -gram(xs[fs, outer], y_in)
            ys[2, top, top] = pivot
            send(3)

            @pl.when(fed)
            def _():
                arrived(4, fed_from)
                abm[...] = ab[inner] + near_ab[fed_from]
                arrived(5, fed_from)
                dd[inner] = far_d[fed_from]

            @pl.when(merges)
            def _():
                arrived(1, below)
                work[slot, top, beyond] = dd[near, top, beyond] + near_d[below, top, beyond]
                arrived(2, below)
                work[slot, beyond] = dd[near, beyond] + near_d[below, beyond]

            pivot = ys[2, top, top]
            block = next_pivot_block(work, slot, 0, pivot)
            sweep(work, slot, 0, pivot)
            ab[outer] = ab[outer] - gram(ys[0], abm[...])
            dd[inner] = dd[inner] - gram(xs[fs, inner], ys[1])
            ys[2, top, top] = pivot_inverse(block)
            send(4)
            send(5)

            @pl.when(fed)
            def _():
                arrived(6, fed_from)
                ab[inner] = far_ab[fed_from]

            for j in range(1, steps):
                pivot = ys[2, top, top]
                if j + 1 < steps:
                    block = next_pivot_block(work, slot, j, pivot)
                sweep(work, slot, j, pivot)
                if j == 1:
                    found = dot(work[old], abm[...])
                    near_ab[keep] = found
                    ab[inner] = ab[inner] - gram(ys[1], abm[...])
                    tip[...] = tip[...] - gram(abm[:, :k], found)
                if j + 1 < steps:
                    ys[2, top, top] = pivot_inverse(block)
                if j == 1:
                    send(6)

            @pl.when(real)
            def _():
                xs[fs, outer] = ys[0]
                xs[fs, inner] = ys[1]

            @pl.when(jnp.logical_or(sent, s == last + 1))
            def _():
                for v in range(levels):
                    @pl.when(jnp.logical_and(hosting[v], v < s))
                    def _():
                        forward_copy(7, v, 0, 1, me).wait_recv()
                        tip[...] = tip[...] + got_tip[v]

            send(7)

            @pl.when(jnp.logical_and(hosts, s <= last))
            def _():
                far = choose(halves, jnp.minimum(s, last))
                close = 1 - far

                @pl.when(s == 0)
                def _():
                    now = trans[0] * first
                    scaled = weight(0, n) * now
                    xs[0, 0] = -scaled
                    xs[0, 1] = -((weight(1, n) * trans[1]).T)
                    dd[0] = gram(now, scaled)
                    dd[1] = diagonal(innov[1:2, :] + observ[1:2, :])

                y_out = dot(work[slot], xs[s, close])
                ys[0] = y_out
                sends = jnp.logical_and(s < last, choose(sending, jnp.minimum(s, last - 1)))
                target = choose(partners, jnp.minimum(s, last - 1))
                level = jnp.minimum(s, last - 1)
                dd[close, top] = dd[close, top] - gram(xs[s, close, :, top], ys[0])

                @pl.when(sends)
                def _():
                    forward_copy(0, level, close, far, target).start()
                    forward_copy(1, level, close, far, target).start()

                dd[close, beyond] = dd[close, beyond] - gram(xs[s, close, :, beyond], ys[0])

                @pl.when(sends)
                def _():
                    forward_copy(2, level, close, far, target).start()

                @pl.when(s == 0)
                def _():
                    loaded_now = weight(0, k) * effects[0]
                    loaded_next = weight(1, k) * effects[1]
                    abm[:, :k] = gram(trans[1], loaded_next) - loaded_now
                    abm[:, k:] = right[0]
                    ab[0, :, :k] = gram(trans[0] * first, loaded_now)
                    ab[0, :, k:] = jnp.zeros((n, m), F32)
                    ab[1, :, :k] = -loaded_next
                    ab[1, :, k:] = right[1]
                    tip[:, :k] = gram(effects[0], loaded_now) + gram(effects[1], loaded_next)
                    tip[:, k:] = jnp.zeros((k, m), F32)

            @pl.when(s == last + 1)
            def _():
                found = dot(work[slot], ab[1])
                near_ab[last + 1] = found
                tip[...] = tip[...] - gram(ab[1, :, :k], found)

            @pl.when(s == last + 2)
            def _():
                found = dot(work[slot], tip_rhs[...])
                tip_sol[...] = found
                sol[levels, 1] = near_ab[last + 1, :, k:] - dot(near_ab[last + 1, :, :k], found)
                sol[levels, 0] = jnp.zeros((n, m), F32)

        return carry

    lax.fori_loop(0, levels + 3, stage, 0)

    def back_copy(what, v, half, target):
        other = 1 - half
        src = (tip_sol, sol.at[v + 1, other], sol.at[v, other])[what]
        dst = (tip_sol, sol.at[v, other], sol.at[v, half])[what]
        return pltpu.make_async_remote_copy(
            src_ref=src,
            dst_ref=dst,
            send_sem=back_send.at[v, what],
            recv_sem=back_recv.at[what],
            device_id=place(target),
            device_id_type=MESH,
        )

    def back(i, carry):
        v = levels - 1 - i
        half = choose(halves, v)
        hosts = choose(hosting, v)
        waits = choose(sending, v)
        target = choose(partners, v)

        @pl.when(hosts)
        def _():
            back_copy(0, v, half, target).start()
            back_copy(1, v, half, target).start()
            value = near_ab[v, :, k:] - dot(near_ab[v, :, :k], tip_sol[...])
            value = value - dot(xs[v + 1, 0], sol[v + 1, 0])
            sol[v, 1 - half] = value - dot(xs[v + 1, 1], sol[v + 1, 1])
            back_copy(2, v, half, target).start()
            sol[v, half] = sol[v + 1, half]

        @pl.when(waits)
        def _():
            for what in range(3):
                back_copy(what, v, 1 - half, me).wait_recv()

        return carry

    lax.fori_loop(0, levels, back, 0)

    value = near_ab[levels, :, k:] - dot(near_ab[levels, :, :k], tip_sol[...])
    value = value - dot(xs[0, 0], sol[0, 0])
    out[0] = value - dot(xs[0, 1], sol[0, 1])
    out[1] = sol[0, 1]
    tip_out[...] = tip_sol[...]

    for v in range(levels):
        @pl.when(sending[v])
        def _():
            for what in range(8):
                forward_copy(what, v, 1 - halves[v], halves[v], partners[v]).wait_send()

        @pl.when(hosting[v])
        def _():
            for what in range(3):
                back_copy(what, v, halves[v], partners[v]).wait_send()


def body(transition, innovation, observation, effects, prior, right_side, tip_right):
    blocks, n = innovation.shape
    k = prior.shape[0]
    m = right_side.shape[2]
    shorts = lax.axis_size("short")
    total = lax.axis_size(AXES)
    levels = total.bit_length() - 1
    assert blocks == 2 and total == 1 << levels
    vmem = pl.BlockSpec(memory_space=pltpu.VMEM)
    wide = k + m
    return pl.pallas_call(
        functools.partial(kernel, levels, shorts),
        out_shape=(
            jax.ShapeDtypeStruct(right_side.shape, F32),
            jax.ShapeDtypeStruct(tip_right.shape, F32),
        ),
        in_specs=[vmem] * 7,
        out_specs=(vmem, vmem),
        scratch_shapes=[
            pltpu.VMEM((2, n, n), F32),
            pltpu.VMEM((2, n, wide), F32),
            pltpu.VMEM((k, wide), F32),
            pltpu.VMEM((2, n, n), F32),
            pltpu.VMEM((n, wide), F32),
            pltpu.VMEM((levels + 2, 2, n, n), F32),
            pltpu.VMEM((3, n, n), F32),
            pltpu.VMEM((levels, n, n), F32),
            pltpu.VMEM((levels + 3, n, wide), F32),
            pltpu.VMEM((levels, n, n), F32),
            pltpu.VMEM((levels, n, wide), F32),
            pltpu.VMEM((levels, k, wide), F32),
            pltpu.VMEM((levels + 1, 2, n, m), F32),
            pltpu.VMEM((k, m), F32),
            pltpu.VMEM((k, m), F32),
            pltpu.SemaphoreType.DMA((8,)),
            pltpu.SemaphoreType.DMA((levels, 8)),
            pltpu.SemaphoreType.DMA((levels, 3)),
            pltpu.SemaphoreType.DMA((3,)),
        ],
        compiler_params=pltpu.CompilerParams(
            collective_id=0, has_side_effects=True, vmem_limit_bytes=67000000
        ),
        name="arrow_solve",
    )(transition, innovation, observation, effects, prior.reshape(1, k), right_side, tip_right)


def solution(mesh):
    placed = (
        P(AXES, None, None),
        P(AXES, None),
        P(AXES, None),
        P(AXES, None, None),
        P(),
        P(AXES, None, None),
        P(),
    )
    return jax.shard_map(
        body,
        mesh=mesh,
        in_specs=placed,
        out_specs=(P(AXES, None, None), P()),
        check_vma=False,
    )
```

```python
import functools

import jax
import jax.numpy as jnp
from jax import lax
from jax.experimental import pallas as pl
from jax.experimental.pallas import tpu as pltpu
from jax.sharding import PartitionSpec as P

AXES = ("long", "short")
PREC = lax.Precision.HIGHEST
LANES = 128
SUBLANES = 8
MESH = pl.DeviceIdType.MESH
F32 = jnp.float32


def dot(left, right):
    return jnp.dot(left, right, precision=PREC, preferred_element_type=F32)


def gram(left, right):
    return lax.dot_general(
        left, right, (((0,), (0,)), ((), ())), precision=PREC, preferred_element_type=F32
    )


def halve(x):
    high = x.astype(jnp.bfloat16)
    return high, (x - high.astype(F32)).astype(jnp.bfloat16)


def dot_three(left, right):
    high, low = halve(left)
    other_high, other_low = halve(right)
    return jnp.dot(
        jnp.concatenate([low, high, high], axis=1),
        jnp.concatenate([other_high, other_low, other_high], axis=0),
        preferred_element_type=F32,
    )


def gram_three(left, right):
    high, low = halve(left)
    other_high, other_low = halve(right)
    return lax.dot_general(
        jnp.concatenate([low, high, high], axis=0),
        jnp.concatenate([other_high, other_low, other_high], axis=0),
        (((0,), (0,)), ((), ())),
        preferred_element_type=F32,
    )


def inverse_two(a, b, c):
    inv = 1.0 / (a * c - b * b)
    return c * inv, -(b * inv), a * inv


def pivot_four(tiles, first, lane, sub):
    group, row = divmod(first, SUBLANES)
    shape = (SUBLANES, LANES)
    cols = [
        [jnp.broadcast_to(t[:, first + k : first + k + 1], shape) for t in tiles] for k in range(4)
    ]

    def entry(i, k):
        return cols[k][group][row + i : row + i + 1, :]

    a00, a01, a11 = inverse_two(entry(0, 0), entry(0, 1), entry(1, 1))
    b00, b01, b10, b11 = entry(0, 2), entry(0, 3), entry(1, 2), entry(1, 3)
    m00, m01 = a00 * b00 + a01 * b10, a00 * b01 + a01 * b11
    m10, m11 = a01 * b00 + a11 * b10, a01 * b01 + a11 * b11
    s00, s01, s11 = inverse_two(
        entry(2, 2) - (b00 * m00 + b10 * m10),
        entry(2, 3) - (b00 * m01 + b10 * m11),
        entry(3, 3) - (b01 * m01 + b11 * m11),
    )
    u00, u01 = m00 * s00 + m01 * s01, m00 * s01 + m01 * s11
    u10, u11 = m10 * s00 + m11 * s01, m10 * s01 + m11 * s11
    t01 = a01 + (u00 * m10 + u01 * m11)
    pivot_inverse = (
        (a00 + (u00 * m00 + u01 * m01), t01, -u00, -u01),
        (t01, a11 + (u10 * m10 + u11 * m11), -u10, -u11),
        (-u00, -u10, s00, s01),
        (-u01, -u11, s01, s11),
    )
    inside = jnp.logical_and(lane >= first, lane < first + 4)
    rows = [
        jnp.where(
            inside[:1],
            jnp.where(lane[:1] == first + k, 1.0, 0.0),
            tiles[group][row + k : row + k + 1, :],
        )
        for k in range(4)
    ]
    scaled = [
        jnp.broadcast_to(
            (p[0] * rows[0] + p[1] * rows[1]) + (p[2] * rows[2] + p[3] * rows[3]), shape
        )
        for p in pivot_inverse
    ]
    out = []
    for place, tile in enumerate(tiles):
        new = jnp.where(inside, 0.0, tile)
        for k in range(4):
            new = new - cols[k][place] * scaled[k]
        if place == group:
            for k in range(4):
                new = jnp.where(sub == row + k, scaled[k], new)
        out.append(new)
    return out


def pivot_inverse(block):
    lane = lax.broadcasted_iota(jnp.int32, (SUBLANES, LANES), 1)
    sub = lax.broadcasted_iota(jnp.int32, (SUBLANES, LANES), 0)
    tiles = [block[SUBLANES * g : SUBLANES * (g + 1), :] for g in range(LANES // SUBLANES)]
    for first in range(0, LANES, 4):
        tiles = pivot_four(tiles, first, lane, sub)
    return jnp.concatenate(tiles, axis=0)


def span(j):
    return pl.ds(j * LANES, LANES)


def sweep(w, slot, j, pivot):
    here = span(j)
    width = w.shape[1]
    columns = w[slot, :, here]
    w[slot, here, :] = dot(pivot, w[slot, here, :])
    w[slot, here, here] = pivot
    scaled = w[slot, here, :]
    w[slot, :, here] = jnp.zeros((width, LANES), F32)
    w[slot] = w[slot] - dot(columns, scaled)
    w[slot, here, :] = scaled


def next_pivot_block(w, slot, j, pivot):
    after = span(j + 1)
    scaled = dot(pivot, w[slot, span(j), after])
    return w[slot, after, after] - dot(w[slot, after, span(j)], scaled)


def host_side(segment):
    return 1 - lax.rem(segment, 2)


def host_of(level, segment):
    for _ in range(level):
        segment = 2 * segment + host_side(segment)
    return segment


def choose(values, index):
    picked = values[0]
    for k in range(1, len(values)):
        picked = jnp.where(index == k, values[k], picked)
    return picked


def column_of(row, width):
    turned = jnp.broadcast_to(row, (LANES, row.shape[1])).T
    return jnp.concatenate([turned] * (width // LANES), axis=1)


def diagonal(row):
    n = row.shape[1]
    at = lax.broadcasted_iota(jnp.int32, (n, n), 0)
    across = lax.broadcasted_iota(jnp.int32, (n, n), 1)
    return jnp.where(at == across, jnp.broadcast_to(row, (n, n)), 0.0)


def kernel(
    levels, shorts,
    trans, innov, observ, effects, prior, right, tip_right,
    out, tip_out,
    dd, ab, tip, work, abm, xs, ys,
    near_d, near_ab, far_d, far_ab, got_tip, sol, tip_sol, tip_rhs, base,
    send_sem, recv_sem, back_send, back_recv,
):
    n = trans.shape[1]
    k = effects.shape[2]
    m = right.shape[2]
    last = levels
    steps = n // LANES
    me = lax.axis_index("long") * shorts + lax.axis_index("short")

    segs = [me // (1 << v) for v in range(levels + 1)]
    halves = [lax.rem(s, 2) for s in segs]
    active = [host_of(v, segs[v]) == me for v in range(levels + 1)]
    partners = [host_of(v, segs[v] + 1 - 2 * halves[v]) for v in range(levels)]
    hosting = [active[v + 1] for v in range(levels)]
    sending = [jnp.logical_and(active[v], jnp.logical_not(active[v + 1])) for v in range(levels)]

    def place(position):
        return (position // shorts, lax.rem(position, shorts))

    barrier = pltpu.get_barrier_semaphore()
    for v in range(levels):
        @pl.when(active[v])
        def _():
            pl.semaphore_signal(barrier, inc=1, device_id=place(partners[v]), device_id_type=MESH)

    top = pl.ds(0, LANES)
    beyond = pl.ds(LANES, n - LANES)

    def forward_copy(what, v, near, far, target):
        src, dst = (
            lambda: (dd.at[near, top, top], near_d.at[v, top, top]),
            lambda: (dd.at[near, top, beyond], near_d.at[v, top, beyond]),
            lambda: (dd.at[near, beyond], near_d.at[v, beyond]),
            lambda: (xs.at[v + 1, far], xs.at[v + 1, far]),
            lambda: (ab.at[near], near_ab.at[v]),
            lambda: (dd.at[far], far_d.at[v]),
            lambda: (ab.at[far], far_ab.at[v]),
            lambda: (tip, got_tip.at[v]),
        )[what]()
        return pltpu.make_async_remote_copy(
            src_ref=src,
            dst_ref=dst,
            send_sem=send_sem.at[what],
            recv_sem=recv_sem.at[v, what],
            device_id=place(target),
            device_id_type=MESH,
        )

    first = jnp.where(me == 0, 0.0, 1.0).astype(F32)

    def weight(t, width):
        return column_of(innov[t : t + 1, :], width)

    work[0] = diagonal(innov[0:1, :] + observ[0:1, :]) + gram(trans[1], weight(1, n) * trans[1])

    count = active[0].astype(jnp.int32)
    for v in range(1, levels):
        count = count + active[v].astype(jnp.int32)
    pl.semaphore_wait(barrier, count)

    runs_at = [active[0]] + active + [active[last]]
    hosts_at = active + [active[last]] * 2

    def stage(s, carry):
        slot = lax.rem(s, 2)
        old = 1 - slot
        hosts = choose(hosts_at, s)
        merges = jnp.logical_and(hosts, jnp.logical_and(s > 0, s <= last))
        below = jnp.clip(s - 1, 0, last - 1)
        fs = jnp.clip(s - 1, 0, last)
        real = jnp.logical_and(s > 0, s <= last + 1)
        fed = jnp.logical_and(s > 1, s <= last + 1)
        fed_from = jnp.clip(fs - 1, 0, last - 1)
        inner = choose(halves, fs)
        outer = 1 - inner
        sent = jnp.logical_and(s > 0, choose(sending, below))
        sent = jnp.logical_and(sent, s <= last)
        sent_to = choose(partners, below)
        keep = jnp.where(real, jnp.where(fs == 0, last, fs - 1), last + 2)

        def send(what):
            @pl.when(sent)
            def _():
                forward_copy(what, below, outer, inner, sent_to).start()

        def arrived(what, v):
            forward_copy(what, v, 0, 1 - choose(halves, v), me).wait_recv()

        @pl.when(choose(runs_at, s))
        def _():
            near = 1 - choose(halves, below)

            @pl.when(merges)
            def _():
                arrived(0, below)
                work[slot, top, top] = dd[near, top, top] + near_d[below, top, top]

            @pl.when(s == last + 1)
            def _():
                work[slot] = dd[1]

            @pl.when(s == last + 2)
            def _():
                work[slot] = tip[:, :k] + diagonal(prior[...].reshape(1, k))
                tip_rhs[...] = tip[:, k:] + tip_right[...]

            @pl.when(fed)
            def _():
                arrived(3, fed_from)

            pivot = pivot_inverse(work[slot, top, top])
            y_in = dot(work[old], xs[fs, inner])
            ys[1] = y_in
            xs[fs + 1, inner] = -gram(xs[fs, outer], y_in)
            ys[2, top, top] = pivot
            send(3)

            @pl.when(fed)
            def _():
                arrived(4, fed_from)
                abm[...] = ab[inner] + near_ab[fed_from]
                arrived(5, fed_from)
                dd[inner] = far_d[fed_from]

            @pl.when(merges)
            def _():
                arrived(1, below)
                work[slot, top, beyond] = dd[near, top, beyond] + near_d[below, top, beyond]
                arrived(2, below)
                work[slot, beyond] = dd[near, beyond] + near_d[below, beyond]

            pivot = ys[2, top, top]
            block = next_pivot_block(work, slot, 0, pivot)
            sweep(work, slot, 0, pivot)
            ab[outer] = ab[outer] - gram_three(ys[0], abm[...])
            dd[inner] = dd[inner] - gram(xs[fs, inner], ys[1])
            ys[2, top, top] = pivot_inverse(block)
            send(4)
            send(5)

            @pl.when(fed)
            def _():
                arrived(6, fed_from)
                ab[inner] = far_ab[fed_from]

            for j in range(1, steps):
                pivot = ys[2, top, top]
                if j + 1 < steps:
                    block = next_pivot_block(work, slot, j, pivot)
                sweep(work, slot, j, pivot)
                if j == 1:
                    found = dot_three(work[old], abm[...])
                    near_ab[keep] = found
                    ab[inner] = ab[inner] - gram_three(ys[1], abm[...])
                    tip[...] = tip[...] - gram_three(abm[:, :k], found)
                if j + 1 < steps:
                    ys[2, top, top] = pivot_inverse(block)
                if j == 1:
                    send(6)

            @pl.when(real)
            def _():
                xs[fs, outer] = ys[0]
                xs[fs, inner] = ys[1]

            @pl.when(jnp.logical_or(sent, s == last + 1))
            def _():
                for v in range(levels):
                    @pl.when(jnp.logical_and(hosting[v], v < s))
                    def _():
                        forward_copy(7, v, 0, 1, me).wait_recv()
                        tip[...] = tip[...] + got_tip[v]

            send(7)

            @pl.when(jnp.logical_and(hosts, s <= last))
            def _():
                far = choose(halves, jnp.minimum(s, last))
                close = 1 - far

                @pl.when(s == 0)
                def _():
                    now = trans[0] * first
                    scaled = weight(0, n) * now
                    xs[0, 0] = -scaled
                    xs[0, 1] = -((weight(1, n) * trans[1]).T)
                    dd[0] = gram(now, scaled)
                    dd[1] = diagonal(innov[1:2, :] + observ[1:2, :])

                y_out = dot(work[slot], xs[s, close])
                ys[0] = y_out
                sends = jnp.logical_and(s < last, choose(sending, jnp.minimum(s, last - 1)))
                target = choose(partners, jnp.minimum(s, last - 1))
                level = jnp.minimum(s, last - 1)
                dd[close, top] = dd[close, top] - gram(xs[s, close, :, top], ys[0])

                @pl.when(sends)
                def _():
                    forward_copy(0, level, close, far, target).start()
                    forward_copy(1, level, close, far, target).start()

                dd[close, beyond] = dd[close, beyond] - gram(xs[s, close, :, beyond], ys[0])

                @pl.when(sends)
                def _():
                    forward_copy(2, level, close, far, target).start()

                @pl.when(s == 0)
                def _():
                    loaded_now = weight(0, k) * effects[0]
                    loaded_next = weight(1, k) * effects[1]
                    abm[:, :k] = gram_three(trans[1], loaded_next) - loaded_now
                    abm[:, k:] = right[0]
                    ab[0, :, :k] = gram_three(trans[0] * first, loaded_now)
                    ab[0, :, k:] = jnp.zeros((n, m), F32)
                    ab[1, :, :k] = -loaded_next
                    ab[1, :, k:] = right[1]
                    tip[:, :k] = gram_three(effects[0], loaded_now) + gram_three(effects[1], loaded_next)
                    tip[:, k:] = jnp.zeros((k, m), F32)

            @pl.when(s == last + 1)
            def _():
                found = dot_three(work[slot], ab[1])
                near_ab[last + 1] = found
                tip[...] = tip[...] - gram_three(ab[1, :, :k], found)

            @pl.when(s == last + 2)
            def _():
                found = dot_three(work[slot], tip_rhs[...])
                tip_sol[...] = found
                sol[levels, 1] = near_ab[last + 1, :, k:] - dot_three(near_ab[last + 1, :, :k], found)
                sol[levels, 0] = jnp.zeros((n, m), F32)

        return carry

    lax.fori_loop(0, levels + 3, stage, 0)

    def back_copy(what, v, half, target):
        other = 1 - half
        src = (tip_sol, sol.at[v + 1, other], sol.at[v, other])[what]
        dst = (tip_sol, sol.at[v, other], sol.at[v, half])[what]
        return pltpu.make_async_remote_copy(
            src_ref=src,
            dst_ref=dst,
            send_sem=back_send.at[v, what],
            recv_sem=back_recv.at[what],
            device_id=place(target),
            device_id_type=MESH,
        )

    def back(i, carry):
        v = levels - i
        half = choose(halves, v)
        waits = jnp.logical_and(v < levels, choose(sending + [sending[0]], v))
        hosts = jnp.logical_and(v < levels, choose(active[1:] + [active[levels]], v))
        level = jnp.minimum(v, levels - 1)
        lower = jnp.maximum(v - 1, 0)
        lower_half = choose(halves, lower)
        lower_target = choose(partners, lower)
        held = jnp.where(v == 0, levels, v - 1)

        @pl.when(choose(active, v))
        def _():
            @pl.when(waits)
            def _():
                back_copy(0, level, 1 - half, me).wait_recv()

            @pl.when(jnp.logical_or(waits, v == levels))
            def _():
                for w in reversed(range(levels)):
                    @pl.when(w < v)
                    def _():
                        back_copy(0, w, halves[w], partners[w]).start()

            base[...] = near_ab[held, :, k:] - dot_three(near_ab[held, :, :k], tip_sol[...])

            @pl.when(waits)
            def _():
                back_copy(1, level, 1 - half, me).wait_recv()

            @pl.when(hosts)
            def _():
                sol[level, half] = sol[level + 1, half]

            base[...] = base[...] - dot_three(xs[v, half], sol[v, half])

            @pl.when(waits)
            def _():
                back_copy(2, level, 1 - half, me).wait_recv()

            @pl.when(v > 0)
            def _():
                back_copy(1, lower, lower_half, lower_target).start()

            value = base[...] - dot_three(xs[v, 1 - half], sol[v, 1 - half])

            @pl.when(v > 0)
            def _():
                sol[lower, 1 - lower_half] = value
                back_copy(2, lower, lower_half, lower_target).start()

            @pl.when(v == 0)
            def _():
                out[0] = value

        return carry

    lax.fori_loop(0, levels + 1, back, 0)
    out[1] = sol[0, 1]
    tip_out[...] = tip_sol[...]

    for v in range(levels):
        @pl.when(sending[v])
        def _():
            for what in range(8):
                forward_copy(what, v, 1 - halves[v], halves[v], partners[v]).wait_send()

        @pl.when(hosting[v])
        def _():
            for what in range(3):
                back_copy(what, v, halves[v], partners[v]).wait_send()


def body(transition, innovation, observation, effects, prior, right_side, tip_right):
    blocks, n = innovation.shape
    k = prior.shape[0]
    m = right_side.shape[2]
    shorts = lax.axis_size("short")
    total = lax.axis_size(AXES)
    levels = total.bit_length() - 1
    assert blocks == 2 and total == 1 << levels
    vmem = pl.BlockSpec(memory_space=pltpu.VMEM)
    wide = k + m
    return pl.pallas_call(
        functools.partial(kernel, levels, shorts),
        out_shape=(
            jax.ShapeDtypeStruct(right_side.shape, F32),
            jax.ShapeDtypeStruct(tip_right.shape, F32),
        ),
        in_specs=[vmem] * 7,
        out_specs=(vmem, vmem),
        scratch_shapes=[
            pltpu.VMEM((2, n, n), F32),
            pltpu.VMEM((2, n, wide), F32),
            pltpu.VMEM((k, wide), F32),
            pltpu.VMEM((2, n, n), F32),
            pltpu.VMEM((n, wide), F32),
            pltpu.VMEM((levels + 2, 2, n, n), F32),
            pltpu.VMEM((3, n, n), F32),
            pltpu.VMEM((levels, n, n), F32),
            pltpu.VMEM((levels + 3, n, wide), F32),
            pltpu.VMEM((levels, n, n), F32),
            pltpu.VMEM((levels, n, wide), F32),
            pltpu.VMEM((levels, k, wide), F32),
            pltpu.VMEM((levels + 1, 2, n, m), F32),
            pltpu.VMEM((k, m), F32),
            pltpu.VMEM((k, m), F32),
            pltpu.VMEM((n, m), F32),
            pltpu.SemaphoreType.DMA((8,)),
            pltpu.SemaphoreType.DMA((levels, 8)),
            pltpu.SemaphoreType.DMA((levels, 3)),
            pltpu.SemaphoreType.DMA((3,)),
        ],
        compiler_params=pltpu.CompilerParams(
            collective_id=0, has_side_effects=True, vmem_limit_bytes=67000000
        ),
        name="arrow_solve",
    )(transition, innovation, observation, effects, prior, right_side, tip_right)


def solution(mesh):
    placed = (
        P(AXES, None, None),
        P(AXES, None),
        P(AXES, None),
        P(AXES, None, None),
        P(),
        P(AXES, None, None),
        P(),
    )
    return jax.shard_map(
        body,
        mesh=mesh,
        in_specs=placed,
        out_specs=(P(AXES, None, None), P()),
        check_vma=False,
    )
```

```python
import functools

import jax
import jax.numpy as jnp
from jax import lax
from jax.experimental import pallas as pl
from jax.experimental.pallas import tpu as pltpu
from jax.sharding import PartitionSpec as P

AXES = ("long", "short")
PREC = lax.Precision.HIGHEST
LANES = 128
SUBLANES = 8
MESH = pl.DeviceIdType.MESH
F32 = jnp.float32


def dot(left, right):
    return jnp.dot(left, right, precision=PREC, preferred_element_type=F32)


def gram(left, right):
    return lax.dot_general(
        left, right, (((0,), (0,)), ((), ())), precision=PREC, preferred_element_type=F32
    )


def halve(x):
    high = x.astype(jnp.bfloat16)
    return high, (x - high.astype(F32)).astype(jnp.bfloat16)


def dot_three(left, right):
    high, low = halve(left)
    other_high, other_low = halve(right)
    return jnp.dot(
        jnp.concatenate([low, high, high], axis=1),
        jnp.concatenate([other_high, other_low, other_high], axis=0),
        preferred_element_type=F32,
    )


def gram_three(left, right):
    high, low = halve(left)
    other_high, other_low = halve(right)
    return lax.dot_general(
        jnp.concatenate([low, high, high], axis=0),
        jnp.concatenate([other_high, other_low, other_high], axis=0),
        (((0,), (0,)), ((), ())),
        preferred_element_type=F32,
    )


def inverse_two(a, b, c):
    inv = 1.0 / (a * c - b * b)
    return c * inv, -(b * inv), a * inv


def pivot_four(tiles, first, lane, sub):
    group, row = divmod(first, SUBLANES)
    shape = (SUBLANES, LANES)
    cols = [
        [jnp.broadcast_to(t[:, first + k : first + k + 1], shape) for t in tiles] for k in range(4)
    ]

    def entry(i, k):
        return cols[k][group][row + i : row + i + 1, :]

    a00, a01, a11 = inverse_two(entry(0, 0), entry(0, 1), entry(1, 1))
    b00, b01, b10, b11 = entry(0, 2), entry(0, 3), entry(1, 2), entry(1, 3)
    m00, m01 = a00 * b00 + a01 * b10, a00 * b01 + a01 * b11
    m10, m11 = a01 * b00 + a11 * b10, a01 * b01 + a11 * b11
    s00, s01, s11 = inverse_two(
        entry(2, 2) - (b00 * m00 + b10 * m10),
        entry(2, 3) - (b00 * m01 + b10 * m11),
        entry(3, 3) - (b01 * m01 + b11 * m11),
    )
    u00, u01 = m00 * s00 + m01 * s01, m00 * s01 + m01 * s11
    u10, u11 = m10 * s00 + m11 * s01, m10 * s01 + m11 * s11
    t01 = a01 + (u00 * m10 + u01 * m11)
    pivot_inverse = (
        (a00 + (u00 * m00 + u01 * m01), t01, -u00, -u01),
        (t01, a11 + (u10 * m10 + u11 * m11), -u10, -u11),
        (-u00, -u10, s00, s01),
        (-u01, -u11, s01, s11),
    )
    inside = jnp.logical_and(lane >= first, lane < first + 4)
    rows = [
        jnp.where(
            inside[:1],
            jnp.where(lane[:1] == first + k, 1.0, 0.0),
            tiles[group][row + k : row + k + 1, :],
        )
        for k in range(4)
    ]
    scaled = [
        jnp.broadcast_to(
            (p[0] * rows[0] + p[1] * rows[1]) + (p[2] * rows[2] + p[3] * rows[3]), shape
        )
        for p in pivot_inverse
    ]
    out = []
    for place, tile in enumerate(tiles):
        new = jnp.where(inside, 0.0, tile)
        for k in range(4):
            new = new - cols[k][place] * scaled[k]
        if place == group:
            for k in range(4):
                new = jnp.where(sub == row + k, scaled[k], new)
        out.append(new)
    return out


def pivot_inverse(block):
    lane = lax.broadcasted_iota(jnp.int32, (SUBLANES, LANES), 1)
    sub = lax.broadcasted_iota(jnp.int32, (SUBLANES, LANES), 0)
    tiles = [block[SUBLANES * g : SUBLANES * (g + 1), :] for g in range(LANES // SUBLANES)]
    for first in range(0, LANES, 4):
        tiles = pivot_four(tiles, first, lane, sub)
    return jnp.concatenate(tiles, axis=0)


def span(j):
    return pl.ds(j * LANES, LANES)


def sweep(w, slot, j, pivot):
    here = span(j)
    width = w.shape[1]
    columns = w[slot, :, here]
    w[slot, here, :] = dot_three(pivot, w[slot, here, :])
    w[slot, here, here] = pivot
    scaled = w[slot, here, :]
    w[slot, :, here] = jnp.zeros((width, LANES), F32)
    w[slot] = w[slot] - dot_three(columns, scaled)
    w[slot, here, :] = scaled


def next_pivot_block(w, slot, j, pivot):
    after = span(j + 1)
    scaled = dot_three(pivot, w[slot, span(j), after])
    return w[slot, after, after] - dot_three(w[slot, after, span(j)], scaled)


def host_side(level, segment):
    if level == 0:
        return 1 - lax.rem(segment // 2, 2)
    if level == 1:
        return lax.rem(segment, 2)
    return 1 - lax.rem(segment, 2)


def host_of(level, segment):
    for low in reversed(range(level)):
        segment = 2 * segment + host_side(low, segment)
    return segment


def choose(values, index):
    picked = values[0]
    for k in range(1, len(values)):
        picked = jnp.where(index == k, values[k], picked)
    return picked


def column_of(row, width):
    turned = jnp.broadcast_to(row, (LANES, row.shape[1])).T
    return jnp.concatenate([turned] * (width // LANES), axis=1)


def diagonal(row):
    n = row.shape[1]
    at = lax.broadcasted_iota(jnp.int32, (n, n), 0)
    across = lax.broadcasted_iota(jnp.int32, (n, n), 1)
    return jnp.where(at == across, jnp.broadcast_to(row, (n, n)), 0.0)


def kernel(
    levels, shorts,
    trans, innov, observ, effects, prior, right, tip_right,
    out, tip_out,
    dd, ab, tip, work, abm, xs, ys,
    near_d, near_ab, far_d, far_ab, got_tip, sol, tip_sol, tip_rhs, base,
    send_sem, recv_sem, back_send, back_recv,
):
    n = trans.shape[1]
    k = effects.shape[2]
    m = right.shape[2]
    last = levels
    steps = n // LANES
    me = lax.axis_index("long") * shorts + lax.axis_index("short")

    segs = [me // (1 << v) for v in range(levels + 1)]
    halves = [lax.rem(s, 2) for s in segs]
    active = [host_of(v, segs[v]) == me for v in range(levels + 1)]
    partners = [host_of(v, segs[v] + 1 - 2 * halves[v]) for v in range(levels)]
    hosting = [active[v + 1] for v in range(levels)]
    sending = [jnp.logical_and(active[v], jnp.logical_not(active[v + 1])) for v in range(levels)]

    def place(position):
        return (position // shorts, lax.rem(position, shorts))

    barrier = pltpu.get_barrier_semaphore()
    for v in range(levels):
        @pl.when(active[v])
        def _():
            pl.semaphore_signal(barrier, inc=1, device_id=place(partners[v]), device_id_type=MESH)

    twin = me + 4 * (1 - 2 * halves[2])
    pl.semaphore_signal(barrier, inc=1, device_id=place(twin), device_id_type=MESH)

    top = pl.ds(0, LANES)
    beyond = pl.ds(LANES, n - LANES)

    def forward_copy(what, v, near, far, target):
        src, dst = (
            lambda: (dd.at[near, top, top], near_d.at[v, top, top]),
            lambda: (dd.at[near, top, beyond], near_d.at[v, top, beyond]),
            lambda: (dd.at[near, beyond, beyond], near_d.at[v, beyond, beyond]),
            lambda: (xs.at[v + 1, far], xs.at[v + 1, far]),
            lambda: (ab.at[near], near_ab.at[v]),
            lambda: (dd.at[far, top], far_d.at[v, top]),
            lambda: (ab.at[far], far_ab.at[v]),
            lambda: (tip, got_tip.at[v]),
            lambda: (dd.at[far, beyond, beyond], far_d.at[v, beyond, beyond]),
        )[what]()
        return pltpu.make_async_remote_copy(
            src_ref=src,
            dst_ref=dst,
            send_sem=send_sem.at[what],
            recv_sem=recv_sem.at[v, what],
            device_id=place(target),
            device_id_type=MESH,
        )

    first = jnp.where(me == 0, 0.0, 1.0).astype(F32)

    def weight(t, width):
        return column_of(innov[t : t + 1, :], width)

    work[0] = diagonal(innov[0:1, :] + observ[0:1, :]) + gram(trans[1], weight(1, n) * trans[1])

    count = active[0].astype(jnp.int32)
    for v in range(1, levels):
        count = count + active[v].astype(jnp.int32)
    pl.semaphore_wait(barrier, count + 1)

    crossed_at = [halves[0] < 0] + [halves[v + 1] == halves[v] for v in range(levels)]
    runs_at = [active[0]] + active + [active[last]]
    hosts_at = active + [active[last]] * 2

    def stage(s, carry):
        slot = lax.rem(s, 2)
        old = 1 - slot
        hosts = choose(hosts_at, s)
        merges = jnp.logical_and(hosts, jnp.logical_and(s > 0, s <= last))
        below = jnp.clip(s - 1, 0, last - 1)
        fs = jnp.clip(s - 1, 0, last)
        real = jnp.logical_and(s > 0, s <= last + 1)
        fed = jnp.logical_and(s > 1, s <= last + 1)
        fed_from = jnp.clip(fs - 1, 0, last - 1)
        inner = choose(halves, fs)
        outer = 1 - inner
        crossed = choose(crossed_at, fs)
        role = crossed.astype(jnp.int32)
        mine = jnp.where(crossed, inner, outer)
        other = 1 - mine
        sent = jnp.logical_and(s > 0, choose(sending, below))
        sent = jnp.logical_and(sent, s <= last)
        sent_to = choose(partners, below)
        keep = jnp.where(real, jnp.where(fs == 0, last, fs - 1), last + 2)

        def send(what, also=True):
            @pl.when(jnp.logical_and(sent, also))
            def _():
                forward_copy(what, below, outer, inner, sent_to).start()

        def arrived(what, v):
            forward_copy(what, v, 0, 1 - choose(halves, v), me).wait_recv()

        def take_far(side, v):
            arrived(5, v)
            arrived(8, v)
            dd[side, top] = far_d[v, top]
            dd[side, beyond, beyond] = far_d[v, beyond, beyond]

        @pl.when(choose(runs_at, s))
        def _():
            near = 1 - choose(halves, below)

            @pl.when(merges)
            def _():
                arrived(0, below)
                work[slot, top, top] = dd[near, top, top] + near_d[below, top, top]

            @pl.when(s == last + 1)
            def _():
                work[slot, top] = dd[1, top]
                work[slot, beyond, beyond] = dd[1, beyond, beyond]
                work[slot, beyond, top] = dd[1, top, beyond].T

            @pl.when(s == last + 2)
            def _():
                work[slot] = tip[:, :k] + diagonal(prior[...].reshape(1, k))
                tip_rhs[...] = tip[:, k:] + tip_right[...]

            @pl.when(jnp.logical_and(fed, jnp.logical_not(crossed)))
            def _():
                arrived(3, fed_from)

            pivot = pivot_inverse(work[slot, top, top])
            y_in = dot(work[old], xs[fs, inner])
            ys[1] = y_in
            xs[fs + 1, inner] = -gram(xs[fs, outer], y_in)
            ys[2, top, top] = pivot
            send(3)

            @pl.when(fed)
            def _():
                arrived(4, fed_from)
                abm[...] = ab[other] + near_ab[fed_from]

            @pl.when(jnp.logical_and(jnp.logical_and(fed, s <= last), jnp.logical_not(crossed)))
            def _():
                take_far(inner, fed_from)

            @pl.when(merges)
            def _():
                arrived(1, below)
                edge = dd[near, top, beyond] + near_d[below, top, beyond]
                work[slot, top, beyond] = edge
                work[slot, beyond, top] = edge.T
                arrived(2, below)
                work[slot, beyond, beyond] = dd[near, beyond, beyond] + near_d[below, beyond, beyond]

            pivot = ys[2, top, top]
            block = next_pivot_block(work, slot, 0, pivot)
            sweep(work, slot, 0, pivot)
            ab[mine] = ab[mine] - gram_three(ys[role], abm[...])
            dd[inner, top] = dd[inner, top] - gram(xs[fs, inner, :, top], ys[1])
            dd[inner, beyond, beyond] = dd[inner, beyond, beyond] - gram(
                xs[fs, inner, :, beyond], ys[1, :, beyond]
            )
            ys[2, top, top] = pivot_inverse(block)
            send(5, below < last - 1)
            send(8, below < last - 1)
            send(4, jnp.logical_not(crossed))

            @pl.when(jnp.logical_and(fed, s <= last))
            def _():
                arrived(6, fed_from)
                ab[other] = far_ab[fed_from]

            for j in range(1, steps):
                pivot = ys[2, top, top]
                if j + 1 < steps:
                    block = next_pivot_block(work, slot, j, pivot)
                sweep(work, slot, j, pivot)
                if j == 1:
                    found = dot_three(work[old], abm[...])
                    near_ab[keep] = found
                    ab[other] = ab[other] - gram_three(ys[1 - role], abm[...])
                    tip[...] = tip[...] - gram_three(abm[:, :k], found)
                if j + 1 < steps:
                    ys[2, top, top] = pivot_inverse(block)
                if j == 1:
                    send(4, crossed)
                    send(6, below < last - 1)

            @pl.when(real)
            def _():
                xs[fs, outer] = ys[0]
                xs[fs, inner] = ys[1]

            @pl.when(jnp.logical_or(sent, s == last + 1))
            def _():
                for v in range(levels):
                    @pl.when(jnp.logical_and(hosting[v], v < s))
                    def _():
                        forward_copy(7, v, 0, 1, me).wait_recv()
                        tip[...] = tip[...] + got_tip[v]

            @pl.when(sent)
            def _():
                to = jnp.where(below == 0, twin, sent_to)
                forward_copy(7, below, outer, inner, to).start()

            @pl.when(jnp.logical_and(hosts, s <= last))
            def _():
                far = choose(halves, jnp.minimum(s, last))
                close = 1 - far

                @pl.when(s == 0)
                def _():
                    now = trans[0] * first
                    scaled = weight(0, n) * now
                    xs[0, 0] = -scaled
                    xs[0, 1] = -((weight(1, n) * trans[1]).T)
                    dd[0] = gram(now, scaled)
                    dd[1] = diagonal(innov[1:2, :] + observ[1:2, :])

                @pl.when(jnp.logical_and(s > 0, choose(crossed_at, jnp.minimum(s, last))))
                def _():
                    arrived(3, below)
                    take_far(close, below)

                y_out = dot(work[slot], xs[s, close])
                ys[0] = y_out
                sends = jnp.logical_and(s < last, choose(sending, jnp.minimum(s, last - 1)))
                target = choose(partners, jnp.minimum(s, last - 1))
                level = jnp.minimum(s, last - 1)
                dd[close, top] = dd[close, top] - gram(xs[s, close, :, top], ys[0])

                @pl.when(sends)
                def _():
                    forward_copy(0, level, close, far, target).start()
                    forward_copy(1, level, close, far, target).start()

                dd[close, beyond, beyond] = dd[close, beyond, beyond] - gram(
                    xs[s, close, :, beyond], ys[0, :, beyond]
                )

                @pl.when(sends)
                def _():
                    forward_copy(2, level, close, far, target).start()

                @pl.when(s == 0)
                def _():
                    loaded_now = weight(0, k) * effects[0]
                    loaded_next = weight(1, k) * effects[1]
                    abm[:, :k] = gram_three(trans[1], loaded_next) - loaded_now
                    abm[:, k:] = right[0]
                    ab[0, :, :k] = gram_three(trans[0] * first, loaded_now)
                    ab[0, :, k:] = jnp.zeros((n, m), F32)
                    ab[1, :, :k] = -loaded_next
                    ab[1, :, k:] = right[1]
                    tip[:, :k] = gram_three(effects[0], loaded_now) + gram_three(effects[1], loaded_next)
                    tip[:, k:] = jnp.zeros((k, m), F32)

            @pl.when(s == last + 1)
            def _():
                found = dot_three(work[slot], ab[1])
                near_ab[last + 1] = found
                tip[...] = tip[...] - gram_three(ab[1, :, :k], found)

            @pl.when(s == last + 2)
            def _():
                found = dot_three(work[slot], tip_rhs[...])
                tip_sol[...] = found
                sol[levels, 1] = near_ab[last + 1, :, k:] - dot_three(near_ab[last + 1, :, :k], found)
                sol[levels, 0] = jnp.zeros((n, m), F32)

        return carry

    lax.fori_loop(0, levels + 3, stage, 0)

    def back_copy(what, v, half, target):
        other = 1 - half
        src = (tip_sol, sol.at[v + 1, other], sol.at[v, other])[what]
        dst = (tip_sol, sol.at[v, other], sol.at[v, half])[what]
        return pltpu.make_async_remote_copy(
            src_ref=src,
            dst_ref=dst,
            send_sem=back_send.at[v, what],
            recv_sem=back_recv.at[what],
            device_id=place(target),
            device_id_type=MESH,
        )

    def back(i, carry):
        v = levels - i
        half = choose(halves, v)
        waits = jnp.logical_and(v < levels, choose(sending + [sending[0]], v))
        hosts = jnp.logical_and(v < levels, choose(active[1:] + [active[levels]], v))
        level = jnp.minimum(v, levels - 1)
        lower = jnp.maximum(v - 1, 0)
        lower_half = choose(halves, lower)
        lower_target = choose(partners, lower)
        held = jnp.where(v == 0, levels, v - 1)

        @pl.when(choose(active, v))
        def _():
            @pl.when(waits)
            def _():
                back_copy(0, level, 1 - half, me).wait_recv()

            @pl.when(jnp.logical_or(waits, v == levels))
            def _():
                for w in reversed(range(levels)):
                    @pl.when(w < v)
                    def _():
                        back_copy(0, w, halves[w], partners[w]).start()

            base[...] = near_ab[held, :, k:] - dot_three(near_ab[held, :, :k], tip_sol[...])

            @pl.when(waits)
            def _():
                back_copy(1, level, 1 - half, me).wait_recv()

            @pl.when(hosts)
            def _():
                sol[level, half] = sol[level + 1, half]

            base[...] = base[...] - dot_three(xs[v, half], sol[v, half])

            @pl.when(waits)
            def _():
                back_copy(2, level, 1 - half, me).wait_recv()

            @pl.when(v > 0)
            def _():
                back_copy(1, lower, lower_half, lower_target).start()

            value = base[...] - dot_three(xs[v, 1 - half], sol[v, 1 - half])

            @pl.when(v > 0)
            def _():
                sol[lower, 1 - lower_half] = value
                back_copy(2, lower, lower_half, lower_target).start()

            @pl.when(v == 0)
            def _():
                out[0] = value

        return carry

    lax.fori_loop(0, levels + 1, back, 0)
    out[1] = sol[0, 1]
    tip_out[...] = tip_sol[...]

    for v in range(levels):
        @pl.when(sending[v])
        def _():
            for what in (range(9) if v < levels - 1 else (0, 1, 2, 3, 4, 7)):
                forward_copy(what, v, 1 - halves[v], halves[v], partners[v]).wait_send()

        @pl.when(hosting[v])
        def _():
            for what in range(3):
                back_copy(what, v, halves[v], partners[v]).wait_send()


def body(transition, innovation, observation, effects, prior, right_side, tip_right):
    blocks, n = innovation.shape
    k = prior.shape[0]
    m = right_side.shape[2]
    shorts = lax.axis_size("short")
    total = lax.axis_size(AXES)
    levels = total.bit_length() - 1
    assert blocks == 2 and total == 1 << levels
    vmem = pl.BlockSpec(memory_space=pltpu.VMEM)
    wide = k + m
    return pl.pallas_call(
        functools.partial(kernel, levels, shorts),
        out_shape=(
            jax.ShapeDtypeStruct(right_side.shape, F32),
            jax.ShapeDtypeStruct(tip_right.shape, F32),
        ),
        in_specs=[vmem] * 7,
        out_specs=(vmem, vmem),
        scratch_shapes=[
            pltpu.VMEM((2, n, n), F32),
            pltpu.VMEM((2, n, wide), F32),
            pltpu.VMEM((k, wide), F32),
            pltpu.VMEM((2, n, n), F32),
            pltpu.VMEM((n, wide), F32),
            pltpu.VMEM((levels + 2, 2, n, n), F32),
            pltpu.VMEM((3, n, n), F32),
            pltpu.VMEM((levels, n, n), F32),
            pltpu.VMEM((levels + 3, n, wide), F32),
            pltpu.VMEM((levels, n, n), F32),
            pltpu.VMEM((levels, n, wide), F32),
            pltpu.VMEM((levels, k, wide), F32),
            pltpu.VMEM((levels + 1, 2, n, m), F32),
            pltpu.VMEM((k, m), F32),
            pltpu.VMEM((k, m), F32),
            pltpu.VMEM((n, m), F32),
            pltpu.SemaphoreType.DMA((9,)),
            pltpu.SemaphoreType.DMA((levels, 9)),
            pltpu.SemaphoreType.DMA((levels, 3)),
            pltpu.SemaphoreType.DMA((3,)),
        ],
        compiler_params=pltpu.CompilerParams(
            collective_id=0, has_side_effects=True, vmem_limit_bytes=67000000
        ),
        name="arrow_solve",
    )(transition, innovation, observation, effects, prior, right_side, tip_right)


def solution(mesh):
    placed = (
        P(AXES, None, None),
        P(AXES, None),
        P(AXES, None),
        P(AXES, None, None),
        P(),
        P(AXES, None, None),
        P(),
    )
    return jax.shard_map(
        body,
        mesh=mesh,
        in_specs=placed,
        out_specs=(P(AXES, None, None), P()),
        check_vma=False,
    )
```

```python
import functools

import jax
import jax.numpy as jnp
from jax import lax
from jax.experimental import pallas as pl
from jax.experimental.pallas import tpu as pltpu
from jax.sharding import PartitionSpec as P

AXES = ("long", "short")
PREC = lax.Precision.HIGHEST
LANES = 128
SUBLANES = 8
MESH = pl.DeviceIdType.MESH
F32 = jnp.float32


def dot(left, right):
    return jnp.dot(left, right, precision=PREC, preferred_element_type=F32)


def gram(left, right):
    return lax.dot_general(
        left, right, (((0,), (0,)), ((), ())), precision=PREC, preferred_element_type=F32
    )


def halve(x):
    high = x.astype(jnp.bfloat16)
    return high, (x - high.astype(F32)).astype(jnp.bfloat16)


def dot_three(left, right):
    high, low = halve(left)
    other_high, other_low = halve(right)
    return jnp.dot(
        jnp.concatenate([low, high, high], axis=1),
        jnp.concatenate([other_high, other_low, other_high], axis=0),
        preferred_element_type=F32,
    )


def gram_three(left, right):
    high, low = halve(left)
    other_high, other_low = halve(right)
    return lax.dot_general(
        jnp.concatenate([low, high, high], axis=0),
        jnp.concatenate([other_high, other_low, other_high], axis=0),
        (((0,), (0,)), ((), ())),
        preferred_element_type=F32,
    )


def inverse_two(a, b, c):
    inv = 1.0 / (a * c - b * b)
    return c * inv, -(b * inv), a * inv


def pivot_four(tiles, first, lane, sub):
    group, row = divmod(first, SUBLANES)
    shape = (SUBLANES, LANES)
    cols = [
        [jnp.broadcast_to(t[:, first + k : first + k + 1], shape) for t in tiles] for k in range(4)
    ]

    def entry(i, k):
        return cols[k][group][row + i : row + i + 1, :]

    a00, a01, a11 = inverse_two(entry(0, 0), entry(0, 1), entry(1, 1))
    b00, b01, b10, b11 = entry(0, 2), entry(0, 3), entry(1, 2), entry(1, 3)
    m00, m01 = a00 * b00 + a01 * b10, a00 * b01 + a01 * b11
    m10, m11 = a01 * b00 + a11 * b10, a01 * b01 + a11 * b11
    s00, s01, s11 = inverse_two(
        entry(2, 2) - (b00 * m00 + b10 * m10),
        entry(2, 3) - (b00 * m01 + b10 * m11),
        entry(3, 3) - (b01 * m01 + b11 * m11),
    )
    u00, u01 = m00 * s00 + m01 * s01, m00 * s01 + m01 * s11
    u10, u11 = m10 * s00 + m11 * s01, m10 * s01 + m11 * s11
    t01 = a01 + (u00 * m10 + u01 * m11)
    pivot_inverse = (
        (a00 + (u00 * m00 + u01 * m01), t01, -u00, -u01),
        (t01, a11 + (u10 * m10 + u11 * m11), -u10, -u11),
        (-u00, -u10, s00, s01),
        (-u01, -u11, s01, s11),
    )
    inside = jnp.logical_and(lane >= first, lane < first + 4)
    rows = [
        jnp.where(
            inside[:1],
            jnp.where(lane[:1] == first + k, 1.0, 0.0),
            tiles[group][row + k : row + k + 1, :],
        )
        for k in range(4)
    ]
    scaled = [
        jnp.broadcast_to(
            (p[0] * rows[0] + p[1] * rows[1]) + (p[2] * rows[2] + p[3] * rows[3]), shape
        )
        for p in pivot_inverse
    ]
    out = []
    for place, tile in enumerate(tiles):
        new = jnp.where(inside, 0.0, tile)
        for k in range(4):
            new = new - cols[k][place] * scaled[k]
        if place == group:
            for k in range(4):
                new = jnp.where(sub == row + k, scaled[k], new)
        out.append(new)
    return out


def pivot_inverse(block):
    lane = lax.broadcasted_iota(jnp.int32, (SUBLANES, LANES), 1)
    sub = lax.broadcasted_iota(jnp.int32, (SUBLANES, LANES), 0)
    tiles = [block[SUBLANES * g : SUBLANES * (g + 1), :] for g in range(LANES // SUBLANES)]
    for first in range(0, LANES, 4):
        tiles = pivot_four(tiles, first, lane, sub)
    return jnp.concatenate(tiles, axis=0)


def span(j):
    return pl.ds(j * LANES, LANES)


def sweep(w, slot, j, pivot):
    here = span(j)
    width = w.shape[1]
    columns = w[slot, :, here]
    w[slot, here, :] = dot_three(pivot, w[slot, here, :])
    w[slot, here, here] = pivot
    scaled = w[slot, here, :]
    w[slot, :, here] = jnp.zeros((width, LANES), F32)
    w[slot] = w[slot] - dot_three(columns, scaled)
    w[slot, here, :] = scaled


def next_pivot_block(w, slot, j, pivot):
    after = span(j + 1)
    scaled = dot_three(pivot, w[slot, span(j), after])
    return w[slot, after, after] - dot_three(w[slot, after, span(j)], scaled)


def host_side(level, segment):
    if level == 0:
        return 1 - lax.rem(segment // 2, 2)
    if level == 1:
        return lax.rem(segment, 2)
    return 1 - lax.rem(segment, 2)


def host_of(level, segment):
    for low in reversed(range(level)):
        segment = 2 * segment + host_side(low, segment)
    return segment


def choose(values, index):
    picked = values[0]
    for k in range(1, len(values)):
        picked = jnp.where(index == k, values[k], picked)
    return picked


def column_of(row, width):
    turned = jnp.broadcast_to(row, (LANES, row.shape[1])).T
    return jnp.concatenate([turned] * (width // LANES), axis=1)


def diagonal(row):
    n = row.shape[1]
    at = lax.broadcasted_iota(jnp.int32, (n, n), 0)
    across = lax.broadcasted_iota(jnp.int32, (n, n), 1)
    return jnp.where(at == across, jnp.broadcast_to(row, (n, n)), 0.0)


def kernel(
    levels, shorts,
    trans, innov, observ, effects, prior, right, tip_right,
    out, tip_out,
    dd, ab, tip, work, abm, xs, ys,
    near_d, near_ab, far_d, far_ab, got_tip, sol, tip_sol, tip_rhs, base,
    send_sem, recv_sem, back_send, back_recv,
):
    n = trans.shape[1]
    k = effects.shape[2]
    m = right.shape[2]
    last = levels
    steps = n // LANES
    me = lax.axis_index("long") * shorts + lax.axis_index("short")

    segs = [me // (1 << v) for v in range(levels + 1)]
    halves = [lax.rem(s, 2) for s in segs]
    active = [host_of(v, segs[v]) == me for v in range(levels + 1)]
    partners = [host_of(v, segs[v] + 1 - 2 * halves[v]) for v in range(levels)]
    hosting = [active[v + 1] for v in range(levels)]
    sending = [jnp.logical_and(active[v], jnp.logical_not(active[v + 1])) for v in range(levels)]

    def place(position):
        return (position // shorts, lax.rem(position, shorts))

    barrier = pltpu.get_barrier_semaphore()
    for v in range(levels):
        @pl.when(active[v])
        def _():
            pl.semaphore_signal(barrier, inc=1, device_id=place(partners[v]), device_id_type=MESH)

    twin = me + 4 * (1 - 2 * halves[2])
    pl.semaphore_signal(barrier, inc=1, device_id=place(twin), device_id_type=MESH)

    top = pl.ds(0, LANES)
    beyond = pl.ds(LANES, n - LANES)

    def forward_copy(what, v, near, far, target):
        src, dst = (
            lambda: (dd.at[near, top, top], near_d.at[v, top, top]),
            lambda: (dd.at[near, top, beyond], near_d.at[v, top, beyond]),
            lambda: (dd.at[near, beyond, beyond], near_d.at[v, beyond, beyond]),
            lambda: (xs.at[v + 1, far], xs.at[v + 1, far]),
            lambda: (ab.at[near], near_ab.at[v]),
            lambda: (dd.at[far, top], far_d.at[v, top]),
            lambda: (ab.at[far], far_ab.at[v]),
            lambda: (tip, got_tip.at[v]),
            lambda: (dd.at[far, beyond, beyond], far_d.at[v, beyond, beyond]),
        )[what]()
        return pltpu.make_async_remote_copy(
            src_ref=src,
            dst_ref=dst,
            send_sem=send_sem.at[what],
            recv_sem=recv_sem.at[v, what],
            device_id=place(target),
            device_id_type=MESH,
        )

    first = jnp.where(me == 0, 0.0, 1.0).astype(F32)

    def weight(t, width):
        return column_of(innov[t : t + 1, :], width)

    work[0] = diagonal(innov[0:1, :] + observ[0:1, :]) + gram(trans[1], weight(1, n) * trans[1])

    count = active[0].astype(jnp.int32)
    for v in range(1, levels):
        count = count + active[v].astype(jnp.int32)
    pl.semaphore_wait(barrier, count + 1)

    crossed_at = [halves[0] < 0] + [halves[v + 1] == halves[v] for v in range(levels)]
    runs_at = [active[0]] + active + [active[last]]
    hosts_at = active + [active[last]] * 2

    def stage(s, carry):
        slot = lax.rem(s, 2)
        old = 1 - slot
        hosts = choose(hosts_at, s)
        merges = jnp.logical_and(hosts, jnp.logical_and(s > 0, s <= last))
        below = jnp.clip(s - 1, 0, last - 1)
        fs = jnp.clip(s - 1, 0, last)
        real = jnp.logical_and(s > 0, s <= last + 1)
        fed = jnp.logical_and(s > 1, s <= last + 1)
        fed_from = jnp.clip(fs - 1, 0, last - 1)
        inner = choose(halves, fs)
        outer = 1 - inner
        crossed = choose(crossed_at, fs)
        role = crossed.astype(jnp.int32)
        mine = jnp.where(crossed, inner, outer)
        other = 1 - mine
        sent = jnp.logical_and(s > 0, choose(sending, below))
        sent = jnp.logical_and(sent, s <= last)
        sent_to = choose(partners, below)
        keep = jnp.where(real, jnp.where(fs == 0, last, fs - 1), last + 2)

        def send(what, also=True):
            @pl.when(jnp.logical_and(sent, also))
            def _():
                forward_copy(what, below, outer, inner, sent_to).start()

        def arrived(what, v):
            forward_copy(what, v, 0, 1 - choose(halves, v), me).wait_recv()

        def take_far(side, v):
            arrived(5, v)
            arrived(8, v)
            dd[side, top] = far_d[v, top]
            dd[side, beyond, beyond] = far_d[v, beyond, beyond]

        @pl.when(choose(runs_at, s))
        def _():
            near = 1 - choose(halves, below)

            @pl.when(merges)
            def _():
                arrived(0, below)
                work[slot, top, top] = dd[near, top, top] + near_d[below, top, top]

            @pl.when(s == last + 1)
            def _():
                work[slot, top] = dd[1, top]
                work[slot, beyond, beyond] = dd[1, beyond, beyond]
                work[slot, beyond, top] = dd[1, top, beyond].T

            @pl.when(s == last + 2)
            def _():
                work[slot] = tip[:, :k] + diagonal(prior[...].reshape(1, k))
                tip_rhs[...] = tip[:, k:] + tip_right[...]

            @pl.when(jnp.logical_and(fed, jnp.logical_not(crossed)))
            def _():
                arrived(3, fed_from)

            pivot = pivot_inverse(work[slot, top, top])
            y_in = dot(work[old], xs[fs, inner])
            ys[1] = y_in
            xs[fs + 1, inner] = -gram(xs[fs, outer], y_in)
            ys[2, top, top] = pivot
            send(3)

            @pl.when(fed)
            def _():
                arrived(4, fed_from)
                abm[...] = ab[other] + near_ab[fed_from]

            @pl.when(jnp.logical_and(jnp.logical_and(fed, s <= last), jnp.logical_not(crossed)))
            def _():
                take_far(inner, fed_from)

            @pl.when(merges)
            def _():
                arrived(1, below)
                edge = dd[near, top, beyond] + near_d[below, top, beyond]
                work[slot, top, beyond] = edge
                work[slot, beyond, top] = edge.T
                arrived(2, below)
                work[slot, beyond, beyond] = dd[near, beyond, beyond] + near_d[below, beyond, beyond]

            pivot = ys[2, top, top]
            block = next_pivot_block(work, slot, 0, pivot)
            sweep(work, slot, 0, pivot)
            ab[mine] = ab[mine] - gram_three(ys[role], abm[...])
            dd[inner, top] = dd[inner, top] - gram(xs[fs, inner, :, top], ys[1])
            dd[inner, beyond, beyond] = dd[inner, beyond, beyond] - gram(
                xs[fs, inner, :, beyond], ys[1, :, beyond]
            )
            ys[2, top, top] = pivot_inverse(block)
            send(5, below < last - 1)
            send(8, below < last - 1)
            send(4, jnp.logical_not(crossed))

            @pl.when(jnp.logical_and(fed, s <= last))
            def _():
                arrived(6, fed_from)
                ab[other] = far_ab[fed_from]

            for j in range(1, steps):
                pivot = ys[2, top, top]
                if j + 1 < steps:
                    block = next_pivot_block(work, slot, j, pivot)
                sweep(work, slot, j, pivot)
                if j == 1:
                    found = dot_three(work[old], abm[...])
                    near_ab[keep] = found
                    ab[other] = ab[other] - gram_three(ys[1 - role], abm[...])
                    tip[...] = tip[...] - gram_three(abm[:, :k], found)
                if j + 1 < steps:
                    ys[2, top, top] = pivot_inverse(block)
                if j == 1:
                    send(4, crossed)
                    send(6, below < last - 1)

            @pl.when(real)
            def _():
                xs[fs, outer] = ys[0]
                xs[fs, inner] = ys[1]

            @pl.when(jnp.logical_or(sent, s == last + 1))
            def _():
                for v in range(levels):
                    @pl.when(jnp.logical_and(hosting[v], v < s))
                    def _():
                        forward_copy(7, v, 0, 1, me).wait_recv()
                        tip[...] = tip[...] + got_tip[v]

            @pl.when(sent)
            def _():
                to = jnp.where(below == 0, twin, sent_to)
                forward_copy(7, below, outer, inner, to).start()

            @pl.when(jnp.logical_and(hosts, s <= last))
            def _():
                far = choose(halves, jnp.minimum(s, last))
                close = 1 - far

                @pl.when(s == 0)
                def _():
                    now = trans[0] * first
                    scaled = weight(0, n) * now
                    xs[0, 0] = -scaled
                    xs[0, 1] = -((weight(1, n) * trans[1]).T)
                    dd[0] = gram(now, scaled)
                    dd[1] = diagonal(innov[1:2, :] + observ[1:2, :])

                @pl.when(jnp.logical_and(s > 0, choose(crossed_at, jnp.minimum(s, last))))
                def _():
                    arrived(3, below)
                    take_far(close, below)

                y_out = dot(work[slot], xs[s, close])
                ys[0] = y_out
                sends = jnp.logical_and(s < last, choose(sending, jnp.minimum(s, last - 1)))
                target = choose(partners, jnp.minimum(s, last - 1))
                level = jnp.minimum(s, last - 1)
                dd[close, top] = dd[close, top] - gram(xs[s, close, :, top], ys[0])

                @pl.when(sends)
                def _():
                    forward_copy(0, level, close, far, target).start()
                    forward_copy(1, level, close, far, target).start()

                dd[close, beyond, beyond] = dd[close, beyond, beyond] - gram(
                    xs[s, close, :, beyond], ys[0, :, beyond]
                )

                @pl.when(sends)
                def _():
                    forward_copy(2, level, close, far, target).start()

                @pl.when(s == 0)
                def _():
                    loaded_now = weight(0, k) * effects[0]
                    loaded_next = weight(1, k) * effects[1]
                    abm[:, :k] = gram_three(trans[1], loaded_next) - loaded_now
                    abm[:, k:] = right[0]
                    ab[0, :, :k] = gram_three(trans[0] * first, loaded_now)
                    ab[0, :, k:] = jnp.zeros((n, m), F32)
                    ab[1, :, :k] = -loaded_next
                    ab[1, :, k:] = right[1]
                    tip[:, :k] = gram_three(effects[0], loaded_now) + gram_three(effects[1], loaded_next)
                    tip[:, k:] = jnp.zeros((k, m), F32)

            @pl.when(s == last + 1)
            def _():
                found = dot_three(work[slot], ab[1])
                near_ab[last + 1] = found
                tip[...] = tip[...] - gram_three(ab[1, :, :k], found)

            @pl.when(s == last + 2)
            def _():
                found = dot_three(work[slot], tip_rhs[...])
                tip_sol[...] = found
                sol[levels, 1] = near_ab[last + 1, :, k:] - dot_three(near_ab[last + 1, :, :k], found)
                sol[levels, 0] = jnp.zeros((n, m), F32)

        return carry

    lax.fori_loop(0, levels + 3, stage, 0)

    def back_copy(what, v, half, target):
        other = 1 - half
        src = (tip_sol, sol.at[v + 1, other], sol.at[v, other])[what]
        dst = (tip_sol, sol.at[v, other], sol.at[v, half])[what]
        return pltpu.make_async_remote_copy(
            src_ref=src,
            dst_ref=dst,
            send_sem=back_send.at[v, what],
            recv_sem=back_recv.at[what],
            device_id=place(target),
            device_id_type=MESH,
        )

    def back(i, carry):
        v = levels - i
        half = choose(halves, v)
        waits = jnp.logical_and(v < levels, choose(sending + [sending[0]], v))
        hosts = jnp.logical_and(v < levels, choose(active[1:] + [active[levels]], v))
        level = jnp.minimum(v, levels - 1)
        lower = jnp.maximum(v - 1, 0)
        lower_half = choose(halves, lower)
        lower_target = choose(partners, lower)
        held = jnp.where(v == 0, levels, v - 1)

        @pl.when(choose(active, v))
        def _():
            @pl.when(waits)
            def _():
                back_copy(0, level, 1 - half, me).wait_recv()

            @pl.when(jnp.logical_or(waits, v == levels))
            def _():
                for w in reversed(range(levels)):
                    @pl.when(w < v)
                    def _():
                        back_copy(0, w, halves[w], partners[w]).start()

            base[...] = near_ab[held, :, k:] - dot_three(near_ab[held, :, :k], tip_sol[...])

            @pl.when(waits)
            def _():
                back_copy(1, level, 1 - half, me).wait_recv()

            @pl.when(hosts)
            def _():
                sol[level, half] = sol[level + 1, half]

            early = half == 1 - lower_half

            @pl.when(jnp.logical_and(v > 0, early))
            def _():
                back_copy(1, lower, lower_half, lower_target).start()

            base[...] = base[...] - dot_three(xs[v, half], sol[v, half])

            @pl.when(waits)
            def _():
                back_copy(2, level, 1 - half, me).wait_recv()

            @pl.when(jnp.logical_and(v > 0, jnp.logical_not(early)))
            def _():
                back_copy(1, lower, lower_half, lower_target).start()

            value = base[...] - dot_three(xs[v, 1 - half], sol[v, 1 - half])

            @pl.when(v > 0)
            def _():
                sol[lower, 1 - lower_half] = value
                back_copy(2, lower, lower_half, lower_target).start()

            @pl.when(v == 0)
            def _():
                out[0] = value

        return carry

    lax.fori_loop(0, levels + 1, back, 0)
    out[1] = sol[0, 1]
    tip_out[...] = tip_sol[...]

    for v in range(levels):
        @pl.when(sending[v])
        def _():
            for what in (range(9) if v < levels - 1 else (0, 1, 2, 3, 4, 7)):
                forward_copy(what, v, 1 - halves[v], halves[v], partners[v]).wait_send()

        @pl.when(hosting[v])
        def _():
            for what in range(3):
                back_copy(what, v, halves[v], partners[v]).wait_send()


def body(transition, innovation, observation, effects, prior, right_side, tip_right):
    blocks, n = innovation.shape
    k = prior.shape[0]
    m = right_side.shape[2]
    shorts = lax.axis_size("short")
    total = lax.axis_size(AXES)
    levels = total.bit_length() - 1
    assert blocks == 2 and total == 1 << levels
    vmem = pl.BlockSpec(memory_space=pltpu.VMEM)
    wide = k + m
    return pl.pallas_call(
        functools.partial(kernel, levels, shorts),
        out_shape=(
            jax.ShapeDtypeStruct(right_side.shape, F32),
            jax.ShapeDtypeStruct(tip_right.shape, F32),
        ),
        in_specs=[vmem] * 7,
        out_specs=(vmem, vmem),
        scratch_shapes=[
            pltpu.VMEM((2, n, n), F32),
            pltpu.VMEM((2, n, wide), F32),
            pltpu.VMEM((k, wide), F32),
            pltpu.VMEM((2, n, n), F32),
            pltpu.VMEM((n, wide), F32),
            pltpu.VMEM((levels + 2, 2, n, n), F32),
            pltpu.VMEM((3, n, n), F32),
            pltpu.VMEM((levels, n, n), F32),
            pltpu.VMEM((levels + 3, n, wide), F32),
            pltpu.VMEM((levels, n, n), F32),
            pltpu.VMEM((levels, n, wide), F32),
            pltpu.VMEM((levels, k, wide), F32),
            pltpu.VMEM((levels + 1, 2, n, m), F32),
            pltpu.VMEM((k, m), F32),
            pltpu.VMEM((k, m), F32),
            pltpu.VMEM((n, m), F32),
            pltpu.SemaphoreType.DMA((9,)),
            pltpu.SemaphoreType.DMA((levels, 9)),
            pltpu.SemaphoreType.DMA((levels, 3)),
            pltpu.SemaphoreType.DMA((3,)),
        ],
        compiler_params=pltpu.CompilerParams(
            collective_id=0, has_side_effects=True, vmem_limit_bytes=67000000
        ),
        name="arrow_solve",
    )(transition, innovation, observation, effects, prior, right_side, tip_right)


def solution(mesh):
    placed = (
        P(AXES, None, None),
        P(AXES, None),
        P(AXES, None),
        P(AXES, None, None),
        P(),
        P(AXES, None, None),
        P(),
    )
    return jax.shard_map(
        body,
        mesh=mesh,
        in_specs=placed,
        out_specs=(P(AXES, None, None), P()),
        check_vma=False,
    )
```
